256 devices in a mesh: branch: 2 (over y_lo), seq: 16 (over z, core), mp: 8 (over x, y_hi).
Axes of the slice: x: 4, y: 4 (y_hi: 2, y_lo: 2; y = y_hi * 2 + y_lo), z: 8, core: 2. Of those that a mesh axis runs over, the one named last changes fastest.
Arguments:
- queries: bfloat16 [2, 16, 2048, 2048], P('branch', 'mp', 'seq'), may hold values from -8 to 8
- keys: bfloat16 [2, 16, 2048, 2048], P('branch', 'mp', 'seq'), may hold values from -8 to 8
- values: bfloat16 [2, 16, 2048, 2048], P('branch', 'mp', 'seq'), may hold values from -6 to 6
- inject: float32 [2, 16], P('branch'), may hold values from 0.2 to 0.8
- keyframes: int32 [2], replicated, may hold values from 0 to 15, as said below
- key_mask: int32 [16, 2], replicated, may hold values 0 or 1
Outputs:
- attended: bfloat16 [2, 16, 2048, 2048], P('branch', 'mp', 'seq')
The draws below stay inside these ranges and needn't reach their ends.
Inputs may be any that keep to these rules, and one draw needn't show every extreme that they name: The keyframes are distinct frames; one of them is the last frame.
All inputs are finite; a program needn't handle non-finite values.
Results may differ from the reference program's by a relative error of at most 0.0061.
Values may be sent and summed in bfloat16 or wider, within the bound.
No kernel may reach another device: no remote copies, remote signals or barrier semaphores. Data moves between devices by JAX's collectives and lax.ppermute only.
A program may use at most 64 MiB of HBM per device.

```python
import math
import jax
import jax.numpy as jnp
from jax import lax

HEAD = 128
NKEY = 2
HEADS = 16
HD = 2048
F = 16
P_SIZE = 2048


def draw_queries(key, part):
    base = jax.random.truncated_normal(jax.random.fold_in(key, 1), -6.0, 6.0, (2, F, P_SIZE, HD), jnp.float32)
    return base.astype(jnp.bfloat16)


def draw_keys(key, part):
    base = jax.random.truncated_normal(jax.random.fold_in(key, 2), -6.0, 6.0, (2, F, P_SIZE, HD), jnp.float32)
    return base.astype(jnp.bfloat16)


def draw_keyframes(key, part):
    earlier = jax.random.permutation(jax.random.fold_in(key, 5), F - 1)[:NKEY - 1].astype(jnp.int32)
    chosen = jnp.concatenate([earlier, jnp.full((1,), F - 1, jnp.int32)])
    return jax.random.permutation(jax.random.fold_in(key, 6), chosen).astype(jnp.int32)


def plant(entries, own_key, least, largest):
    extent = entries.shape
    index_at = [jax.random.randint(jax.random.fold_in(own_key, axis), (), 0, extent[axis]) for axis in range(len(extent))]
    entries = entries.at[tuple(index_at)].set(least)
    longest = extent.index(max(extent))
    index_at[longest] = (index_at[longest] + 1) % extent[longest]
    return entries.at[tuple(index_at)].set(largest)


def steps_of(rng, extent, cuts, smallest, largest):
    def one(position, parts):
        steps = jax.random.uniform(jax.random.fold_in(jax.random.fold_in(rng, 6), position), (parts,), jnp.float32, smallest / len(cuts), largest / len(cuts))
        return jnp.repeat(jnp.exp(steps), extent[position] // parts).reshape((-1,) + (1,) * (len(extent) - position - 1))

    loudness = one(*cuts[0])
    for cut in cuts[1:]:
        loudness = loudness * one(*cut)
    return loudness


def bell_draw(key, extent, spread, most, split=(), held_as=jnp.bfloat16):
    drawn = spread * jax.random.normal(key, extent, jnp.float32)
    if split:
        drawn = drawn * steps_of(key, extent, split, -0.22, 0.18)
    return jnp.clip(drawn, -most, most).astype(held_as)


def setup_inputs(seed: int = 0) -> dict:
    key_list = jax.random.split(jax.random.key(seed), 7)
    queries = draw_queries(jax.random.fold_in(key_list[6], 71), 0)
    keys = draw_keys(jax.random.fold_in(key_list[6], 71), 0)
    values = bell_draw(key_list[2], (2, F, P_SIZE, HD), 1.0, 6.0, ((0, 2), (1, 8), (2, 16)))
    inject = jnp.clip(0.2 + 0.6 * jax.random.uniform(key_list[3], (2, HEADS), jnp.float32) ** steps_of(key_list[3], (2, HEADS), ((0, 2),), -0.2, 0.2), 0.2, 0.8)
    keyframes = draw_keyframes(jax.random.fold_in(key_list[6], 71), 0)
    key_mask = plant((jax.random.randint(key_list[5], (F, NKEY), 0, 2) < 1).astype(jnp.int32), jax.random.fold_in(key_list[5], 1), 0, 1)
    return dict(queries=queries, keys=keys, values=values, inject=inject, keyframes=keyframes, key_mask=key_mask)


NEG_FILL = -1e+30

def blend_branches(source, strength):
    as_float = source.astype(jnp.float32)
    return ((1.0 - strength) * as_float + strength * as_float[::-1]).astype(jnp.bfloat16)

def one_head(query_rows, key_rows, value_rows, valid_keys):
    scores = jnp.dot(query_rows, key_rows.T, preferred_element_type=jnp.float32) * (1.0 / math.sqrt(HEAD))
    scores = jnp.where(valid_keys[None, :], scores, NEG_FILL)
    row_max = lax.optimization_barrier(jnp.max(scores, axis=1, keepdims=True))
    weights = jnp.where(valid_keys[None, :], jnp.exp(scores - row_max), 0.0)
    totals = lax.optimization_barrier(jnp.sum(weights, axis=1, keepdims=True))
    mixed_out = jnp.dot(weights.astype(jnp.bfloat16), value_rows, preferred_element_type=jnp.float32)
    return (mixed_out / totals).astype(jnp.bfloat16)

def by_heads(rows):
    return rows.reshape(rows.shape[0], HEADS, HEAD).transpose(1, 0, 2)

def reference(queries, keys, values, inject, keyframes, key_mask):
    strength = jnp.repeat(inject, HEAD, axis=1)[:, None, None, :]
    mixed_queries = blend_branches(queries, strength)
    mixed_keys = blend_branches(keys, strength)

    def one_frame(flat_index):
        branch = flat_index // F
        frame_index = flat_index % F
        query_rows = mixed_queries[branch, frame_index]
        key_rows = jnp.concatenate([mixed_keys[branch, frame_index], mixed_keys[branch][keyframes].reshape(NKEY * P_SIZE, HD)], axis=0)
        value_rows = jnp.concatenate([values[branch, frame_index], values[branch][keyframes].reshape(NKEY * P_SIZE, HD)], axis=0)
        valid_keys = jnp.concatenate([jnp.ones((P_SIZE,), jnp.bool_), jnp.repeat(key_mask[frame_index] > 0, P_SIZE)])

        def head_step(operands):
            return one_head(operands[0], operands[1], operands[2], valid_keys)
        outputs = lax.map(head_step, (by_heads(query_rows), by_heads(key_rows), by_heads(value_rows)))
        return outputs.transpose(1, 0, 2).reshape(P_SIZE, HD)
    result = lax.map(one_frame, jnp.arange(2 * F, dtype=jnp.int32))
    return result.reshape(2, F, P_SIZE, HD)
```

```python
import functools
import math

import jax
import jax.numpy as jnp
from jax import lax
from jax.experimental import pallas as pl
from jax.experimental.pallas import tpu as pltpu
from jax.sharding import PartitionSpec as P


HEAD = 128
SCALE = math.log2(math.e) / math.sqrt(HEAD)
SAFE = 100.0
BF16 = jnp.bfloat16
F32 = jnp.float32


def blend_kernel(strength_ref, own_ref, partner_ref, *out_refs, heads):
    first = pl.program_id(0) * heads
    for head in range(heads):
        share = strength_ref[0, first + head]
        lanes = slice(head * HEAD, (head + 1) * HEAD)
        mixed = (
            (1.0 - share) * own_ref[:, :, lanes].astype(F32)
            + share * partner_ref[:, :, lanes].astype(F32)
        ).astype(BF16)
        if len(out_refs) == 1:
            out_refs[0][head] = mixed
        else:
            for frame, out_ref in enumerate(out_refs):
                out_ref[head] = mixed[frame]


def blend_heads(strength, own, partner, per_frame, steps=4):
    frames, rows, width = own.shape
    heads = width // HEAD
    group = heads // steps
    block = pl.BlockSpec((frames, rows, group * HEAD), lambda h: (0, 0, h))
    if per_frame:
        out_specs = [pl.BlockSpec((group, rows, HEAD), lambda h: (h, 0, 0))] * frames
        out_shape = [jax.ShapeDtypeStruct((heads, rows, HEAD), BF16)] * frames
    else:
        out_specs = [pl.BlockSpec((group, frames, rows, HEAD), lambda h: (h, 0, 0, 0))]
        out_shape = [jax.ShapeDtypeStruct((heads, frames, rows, HEAD), BF16)]
    return pl.pallas_call(
        functools.partial(blend_kernel, heads=group),
        grid=(steps,),
        in_specs=[pl.BlockSpec(memory_space=pltpu.SMEM), block, block],
        out_specs=out_specs,
        out_shape=out_shape,
        cost_estimate=pl.CostEstimate(
            flops=3 * own.size, bytes_accessed=6 * own.size, transcendentals=0
        ),
        name="blend",
    )(strength, own, partner)


def dot_nt(a, b):
    return lax.dot_general(a, b, (((1,), (1,)), ((), ())), preferred_element_type=F32)


def scaled_split(query):
    scaled = query.astype(F32) * SCALE
    high = scaled.astype(BF16)
    low = (scaled - high.astype(F32)).astype(BF16)
    return jnp.concatenate([high, low], axis=1)


def score_tile(query_pair, key):
    return dot_nt(query_pair, jnp.concatenate([key, key], axis=1))


def with_ones(value):
    return jnp.concatenate([value, jnp.ones_like(value)], axis=1)


def weighted(weights, value):
    return jnp.dot(weights.astype(BF16), with_ones(value), preferred_element_type=F32)


def norm_max(block):
    as_float = block.astype(F32)
    return jnp.max(jnp.sum(as_float * as_float, axis=1))


def is_safe(query_norm, key_norm):
    return query_norm * key_norm * (SCALE * SCALE) <= SAFE * SAFE


def tiles_of(ref, lead, tile):
    blocks, rows = ref.shape[-3], ref.shape[-2]
    step = max(1, tile // rows)
    for start in range(0, blocks, step):
        stop = min(blocks, start + step)
        yield lambda start=start, stop=stop: ref[lead + (slice(start, stop),)].reshape(
            (stop - start) * rows, HEAD
        )


def pairs_of(key_refs, value_refs, lead, tile):
    for key_ref, value_ref in zip(key_refs, value_refs):
        yield from zip(tiles_of(key_ref, lead, tile), tiles_of(value_ref, lead, tile))


def own_kernel(query_ref, key_ref, value_ref, acc_ref, norm_ref, *, tile):
    @pl.when(pl.program_id(0) == 0)
    def _():
        norm_ref[0] = norm_max(key_ref[...].reshape(-1, HEAD))

    query = query_ref[...].reshape(-1, HEAD)

    @pl.when(is_safe(norm_max(query), norm_ref[0]))
    def _():
        pair = scaled_split(query)
        for index, (key, value) in enumerate(pairs_of([key_ref], [value_ref], (), tile)):
            part = weighted(jnp.exp2(score_tile(pair, key())), value())
            acc_ref[...] = part if index == 0 else acc_ref[...] + part


def extra_kernel(
    valid_ref, query_ref, key_ref, value_ref, *refs, tile, pieces, extras
):
    key_extra = refs[:pieces]
    value_extra = refs[pieces : 2 * pieces]
    *acc_in, out_ref, norm_ref, acc_ref, max_ref = refs[2 * pieces :]
    blocks, rows = query_ref.shape[0], query_ref.shape[1]

    @pl.when(pl.program_id(0) == 0)
    def _():
        norm = norm_max(key_ref[...].reshape(-1, HEAD))
        for ref in key_extra:
            norm = jnp.maximum(norm, norm_max(ref[...].reshape(-1, HEAD)))
        norm_ref[0] = norm

    query = query_ref[...].reshape(-1, HEAD)
    safe = is_safe(norm_max(query), norm_ref[0])

    @pl.when(safe)
    def _():
        pair = scaled_split(query)
        if acc_in:
            acc_ref[...] = acc_in[0][...]
        else:
            for index, (key, value) in enumerate(pairs_of([key_ref], [value_ref], (), tile)):
                part = weighted(jnp.exp2(score_tile(pair, key())), value())
                acc_ref[...] = part if index == 0 else acc_ref[...] + part

        def one_extra(slot, carry):
            @pl.when(valid_ref[slot] > 0)
            def _():
                for key, value in pairs_of(key_extra, value_extra, (slot,), tile):
                    acc_ref[...] += weighted(jnp.exp2(score_tile(pair, key())), value())

            return carry

        lax.fori_loop(0, extras, one_extra, 0)
        acc = acc_ref[...]
        out_ref[...] = (acc[:, :HEAD] / acc[:, HEAD:]).astype(BF16).reshape(out_ref.shape)

    @pl.when(jnp.logical_not(safe))
    def _():
        def one_block(block, carry):
            pair = scaled_split(query_ref[block])
            acc_slow = acc_ref.at[pl.ds(0, rows)]

            def step(key, value, first):
                scores = score_tile(pair, key)
                top = jnp.max(scores, axis=1, keepdims=True)
                if first:
                    new_max = top
                else:
                    old_max = max_ref[:, :1]
                    new_max = jnp.maximum(old_max, top)
                part = weighted(jnp.exp2(scores - new_max), value)
                if first:
                    acc_slow[...] = part
                else:
                    acc_slow[...] = acc_slow[...] * jnp.exp2(old_max - new_max) + part
                max_ref[...] = jnp.broadcast_to(new_max, max_ref.shape)

            for index, (key, value) in enumerate(pairs_of([key_ref], [value_ref], (), 512)):
                step(key(), value(), index == 0)

            def one_extra(slot, carry):
                @pl.when(valid_ref[slot] > 0)
                def _():
                    for key, value in pairs_of(key_extra, value_extra, (slot,), 512):
                        step(key(), value(), False)

                return carry

            lax.fori_loop(0, extras, one_extra, 0)
            acc = acc_slow[...]
            out_ref[block] = (acc[:, :HEAD] / acc[:, HEAD:]).astype(BF16)
            return carry

        lax.fori_loop(0, blocks, one_block, 0)


def whole(array):
    return pl.BlockSpec(
        array.shape, lambda i: (0,) * array.ndim, pipeline_mode=pl.Buffered(1)
    )


def frame_of(array, frame):
    blocks, _, rows, width = array.shape
    return pl.BlockSpec(
        (blocks, None, rows, width), lambda i: (0, frame, 0, 0), pipeline_mode=pl.Buffered(1)
    )


def attention_cost(queries, keys):
    return pl.CostEstimate(
        flops=4 * queries * keys * HEAD,
        bytes_accessed=4 * (queries + keys) * HEAD,
        transcendentals=queries * keys,
    )


def attend_own(frame, query, key, value, steps, tile):
    blocks, rows, _ = query.shape
    per_step = blocks // steps
    total = blocks * rows
    return pl.pallas_call(
        functools.partial(own_kernel, tile=tile),
        grid=(steps,),
        in_specs=[
            pl.BlockSpec((per_step, rows, HEAD), lambda i: (i, 0, 0)),
            frame_of(key, frame),
            frame_of(value, frame),
        ],
        out_specs=pl.BlockSpec((per_step * rows, 2 * HEAD), lambda i: (i, 0)),
        out_shape=jax.ShapeDtypeStruct((total, 2 * HEAD), F32),
        scratch_shapes=[pltpu.SMEM((1,), F32)],
        compiler_params=pltpu.CompilerParams(vmem_limit_bytes=24 << 20),
        cost_estimate=attention_cost(total, total),
        name="attend_own",
    )(query, key, value)


def attend_extra(frame, valid, query, key, value, key_extra, value_extra, acc, steps, tile):
    blocks, rows, _ = query.shape
    per_step = blocks // steps
    total = blocks * rows
    pieces = len(key_extra)
    extras = valid.shape[0]
    acc = [] if acc is None else [acc]
    return pl.pallas_call(
        functools.partial(extra_kernel, tile=tile, pieces=pieces, extras=extras),
        grid=(steps,),
        in_specs=[
            pl.BlockSpec(memory_space=pltpu.SMEM),
            pl.BlockSpec((per_step, rows, HEAD), lambda i: (i, 0, 0)),
            frame_of(key, frame),
            frame_of(value, frame),
            *[whole(a) for a in key_extra],
            *[whole(a) for a in value_extra],
            *[pl.BlockSpec((per_step * rows, 2 * HEAD), lambda i: (i, 0)) for _ in acc],
        ],
        out_specs=pl.BlockSpec((per_step, rows, HEAD), lambda i: (i, 0, 0)),
        out_shape=jax.ShapeDtypeStruct((blocks, rows, HEAD), BF16),
        scratch_shapes=[
            pltpu.SMEM((1,), F32),
            pltpu.VMEM((per_step * rows, 2 * HEAD), F32),
            pltpu.VMEM((rows, HEAD), F32),
        ],
        compiler_params=pltpu.CompilerParams(vmem_limit_bytes=24 << 20),
        cost_estimate=attention_cost(total, extras * total),
        name="attend_extra",
    )(valid, query, key, value, *key_extra, *value_extra, *acc)


def cut_kernel(place_ref, keyframes_ref, source_ref, *out_refs, xs):
    blocks, frames = source_ref.shape[:2]
    quarter = blocks // xs
    x = place_ref[0] // 2
    for step, out_ref in enumerate(out_refs, 1):
        start = lax.rem(x + step, xs) * quarter
        for j in range(out_ref.shape[0]):
            slot = lax.rem(keyframes_ref[j], frames)
            for block in range(quarter):
                out_ref[j, block] = source_ref[start + block, slot]


def pick_x_kernel(place_ref, keyframes_ref, source_ref, *refs):
    *got_refs, out_ref = refs
    xs = len(got_refs) + 1
    blocks, frames = source_ref.shape[:2]
    quarter = blocks // xs
    x = place_ref[0] // 2
    for j in range(out_ref.shape[0]):
        keyframe = keyframes_ref[j]
        step = lax.rem(x - keyframe // (2 * frames) + xs, xs)

        @pl.when(step == 0)
        def _():
            slot = lax.rem(keyframe, frames)
            for block in range(quarter):
                out_ref[j, block] = source_ref[x * quarter + block, slot]

        for which, got_ref in enumerate(got_refs, 1):

            @pl.when(step == which)
            def _():
                out_ref[j] = got_ref[j]


def pick_y_kernel(place_ref, keyframes_ref, mine_ref, other_ref, out_ref, *, frames):
    y = lax.rem(place_ref[0], 2)
    for j in range(out_ref.shape[0]):
        same = lax.rem(keyframes_ref[j] // frames, 2) == y

        @pl.when(same)
        def _():
            out_ref[j] = mine_ref[j]

        @pl.when(jnp.logical_not(same))
        def _():
            out_ref[j] = other_ref[j]


def move_call(kernel, out_shapes, place, keyframes, *arrays):
    smem = pl.BlockSpec(memory_space=pltpu.SMEM)
    vmem = pl.BlockSpec(memory_space=pltpu.VMEM)
    moved = sum(a.size for a in arrays) + sum(math.prod(o.shape) for o in out_shapes)
    return pl.pallas_call(
        kernel,
        in_specs=[smem, smem] + [vmem] * len(arrays),
        out_specs=[vmem] * len(out_shapes),
        out_shape=out_shapes,
        cost_estimate=pl.CostEstimate(flops=0, bytes_accessed=2 * moved, transcendentals=0),
    )(place, keyframes, *arrays)


def piece_shape(keyframes, by_frame, xs):
    blocks, _, rows, width = by_frame.shape
    return jax.ShapeDtypeStruct((keyframes.shape[0], blocks // xs, rows, width), BF16)


def cut_pieces(place, keyframes, by_frame, xs):
    return move_call(
        functools.partial(cut_kernel, xs=xs),
        [piece_shape(keyframes, by_frame, xs)] * (xs - 1), place, keyframes, by_frame,
    )


def pick_along_x(place, keyframes, by_frame, got):
    return move_call(
        pick_x_kernel,
        [piece_shape(keyframes, by_frame, len(got) + 1)], place, keyframes, by_frame, *got,
    )[0]


def pick_along_y(place, keyframes, mine, other, frames):
    return move_call(
        functools.partial(pick_y_kernel, frames=frames),
        [jax.ShapeDtypeStruct(mine.shape, BF16)], place, keyframes, mine, other,
    )[0]


def swap_branch(value):
    return lax.ppermute(value, "branch", [(0, 1), (1, 0)])


def to_heads(value):
    return lax.all_to_all(value, "seq", split_axis=0, concat_axis=0, tiled=True)


def shift_x(value, step):
    size = lax.axis_size("mp")
    return lax.ppermute(value, "mp", [(m, (m + 2 * step) % size) for m in range(size)])


def flip_y(value):
    size = lax.axis_size("mp")
    return lax.ppermute(value, "mp", [(m, m ^ 1) for m in range(size)])


def spread_keyframes(by_frame, keyframes):
    place = lax.axis_index("mp").astype(jnp.int32).reshape(1)
    xs = lax.axis_size("mp") // 2
    pieces = cut_pieces(place, keyframes, by_frame, xs)
    got = [shift_x(piece, step) for step, piece in enumerate(pieces, 1)]
    mine = pick_along_x(place, keyframes, by_frame, got)
    other = flip_y(mine)
    mine = pick_along_y(place, keyframes, mine, other, by_frame.shape[1])
    return [mine] + [shift_x(mine, step) for step in range(1, xs)]


def by_head(block):
    frames, rows, width = block.shape
    return block.reshape(frames, rows, width // HEAD, HEAD).transpose(2, 0, 1, 3)


def local(queries, keys, values, inject, keyframes, key_mask):
    queries, keys, values = queries[0], keys[0], values[0]
    frames = queries.shape[0]
    partner_keys = swap_branch(keys)
    partner_queries = swap_branch(queries)

    value_rows = by_head(values)
    value_heads = to_heads(value_rows)
    value_extra = spread_keyframes(value_heads, keyframes)

    (key_rows,) = blend_heads(inject, keys, partner_keys, False)
    key_heads = to_heads(key_rows)
    key_source, *value_extra = lax.optimization_barrier((key_heads, *value_extra))
    key_extra = spread_keyframes(key_source, keyframes)

    query_rows = blend_heads(inject, queries, partner_queries, True)
    query_frames = []
    for f in range(frames):
        query_frames.append(to_heads(query_rows[f]))

    first = lax.axis_index("mp") * frames
    outs = []
    for f in range(frames):
        acc = None
        if f == 0:
            acc = attend_own(f, query_frames[f], key_heads, value_heads, 2, 512)
        valid = lax.dynamic_index_in_dim(key_mask, first + f, 0, keepdims=False)
        out = attend_extra(
            f, valid, query_frames[f], key_heads, value_heads,
            key_extra, value_extra, acc, 2, 512,
        )
        back = to_heads(out)
        heads, rows, _ = back.shape
        outs.append(back.transpose(1, 0, 2).reshape(rows, heads * HEAD))
    return jnp.stack(outs)[None]


def solution(mesh):
    return jax.shard_map(
        local,
        mesh=mesh,
        in_specs=(
            P("branch", "mp", "seq", None),
            P("branch", "mp", "seq", None),
            P("branch", "mp", "seq", None),
            P("branch", None),
            P(),
            P(),
        ),
        out_specs=P("branch", "mp", "seq", None),
        check_vma=False,
    )
```

```python
import functools
import math

import jax
import jax.numpy as jnp
from jax import lax
from jax.experimental import pallas as pl
from jax.experimental.pallas import tpu as pltpu
from jax.sharding import PartitionSpec as P


HEAD = 128
SCALE = math.log2(math.e) / math.sqrt(HEAD)
SAFE = 100.0
LOWEST = -1e30
BF16 = jnp.bfloat16
F32 = jnp.float32


def blend_kernel(strength_ref, own_ref, partner_ref, *out_refs, heads):
    first = pl.program_id(0) * heads
    for head in range(heads):
        share = strength_ref[0, first + head]
        lanes = slice(head * HEAD, (head + 1) * HEAD)
        mixed = (
            (1.0 - share) * own_ref[:, :, lanes].astype(F32)
            + share * partner_ref[:, :, lanes].astype(F32)
        ).astype(BF16)
        if len(out_refs) == 1:
            out_refs[0][head] = mixed
        else:
            for frame, out_ref in enumerate(out_refs):
                out_ref[head] = mixed[frame]


def blend_heads(strength, own, partner, per_frame, steps=2):
    frames, rows, width = own.shape
    heads = width // HEAD
    group = heads // steps
    block = pl.BlockSpec((frames, rows, group * HEAD), lambda h: (0, 0, h))
    if per_frame:
        out_specs = [pl.BlockSpec((group, rows, HEAD), lambda h: (h, 0, 0))] * frames
        out_shape = [jax.ShapeDtypeStruct((heads, rows, HEAD), BF16)] * frames
    else:
        out_specs = [pl.BlockSpec((group, frames, rows, HEAD), lambda h: (h, 0, 0, 0))]
        out_shape = [jax.ShapeDtypeStruct((heads, frames, rows, HEAD), BF16)]
    return pl.pallas_call(
        functools.partial(blend_kernel, heads=group),
        grid=(steps,),
        in_specs=[pl.BlockSpec(memory_space=pltpu.SMEM), block, block],
        out_specs=out_specs,
        out_shape=out_shape,
        cost_estimate=pl.CostEstimate(
            flops=3 * own.size, bytes_accessed=6 * own.size, transcendentals=0
        ),
        name="blend",
    )(strength, own, partner)


def split_kernel(source_ref, out_ref, sem):
    heads = out_ref.shape[0]
    copies = [
        pltpu.make_async_copy(
            source_ref.at[:, :, pl.ds(head * HEAD, HEAD)], out_ref.at[head], sem.at[head]
        )
        for head in range(heads)
    ]
    for copy in copies:
        copy.start()
    for copy in copies:
        copy.wait()


def split_heads(rows):
    frames, count, width = rows.shape
    heads = width // HEAD
    out = jax.ShapeDtypeStruct((heads, frames, count, HEAD), BF16)
    return pl.pallas_call(
        split_kernel,
        grid=(1,),
        in_specs=[pl.BlockSpec(memory_space=pl.ANY)],
        out_specs=whole(out),
        out_shape=out,
        scratch_shapes=[pltpu.SemaphoreType.DMA((heads,))],
        cost_estimate=pl.CostEstimate(flops=0, bytes_accessed=4 * rows.size, transcendentals=0),
        name="split_heads",
    )(rows)


def dot_nt(a, b):
    return lax.dot_general(a, b, (((1,), (1,)), ((), ())), preferred_element_type=F32)


def scaled_split(query):
    scaled = query.astype(F32) * SCALE
    high = scaled.astype(BF16)
    low = (scaled - high.astype(F32)).astype(BF16)
    return jnp.concatenate([high, low], axis=1)


def score_tile(query_pair, key):
    return dot_nt(query_pair, jnp.concatenate([key, key], axis=1))


def with_ones(value):
    return jnp.concatenate([value, jnp.ones_like(value)], axis=1)


def weighted(weights, value):
    return jnp.dot(weights.astype(BF16), with_ones(value), preferred_element_type=F32)


def norm_max(rows):
    rows = rows.reshape(-1, HEAD)
    sums = jnp.dot(rows * rows, jnp.ones((HEAD, HEAD), BF16), preferred_element_type=F32)
    return jnp.max(sums)


def copy_all(sources, target, sem):
    copies = []
    start = 0
    for source in sources:
        blocks = source.shape[0]
        copies.append(
            pltpu.make_async_copy(source, target.at[pl.ds(start, blocks)], sem.at[len(copies)])
        )
        start += blocks
    for copy in copies:
        copy.start()
    return copies


def attend_kernel(valid_ref, query_ref, key_ref, value_ref, *refs, frame, tile, pieces, mode):
    key_extra, value_extra = refs[:pieces], refs[pieces : 2 * pieces]
    acc_in = refs[2 * pieces : 2 * pieces + 1] if mode == "more" else ()
    out_ref, keys, values, acc, top, key_sem, value_sem = refs[2 * pieces + len(acc_in) :]
    parts = keys.shape[0]
    blocks, rows = query_ref.shape[0], query_ref.shape[1]
    step = tile // rows

    key_copies, value_copies = [], []
    for part in range(parts):
        if part == 0:
            key_sources, value_sources = [key_ref.at[:, frame]], [value_ref.at[:, frame]]
        else:
            key_sources = [ref.at[part - 1] for ref in key_extra]
            value_sources = [ref.at[part - 1] for ref in value_extra]
        key_copies += copy_all(key_sources, keys.at[part], key_sem.at[part])
        value_copies += copy_all(value_sources, values.at[part], value_sem.at[part])

    query = query_ref[...].reshape(-1, HEAD)
    query_norm = norm_max(query)
    for copy in key_copies:
        copy.wait()
    key_norm = norm_max(keys[0])
    for part in range(1, parts):
        key_norm = jnp.maximum(key_norm, norm_max(keys[part]))
    safe = query_norm * key_norm * (SCALE * SCALE) <= SAFE * SAFE
    for copy in value_copies:
        copy.wait()

    def tiles(part, first=0, count=blocks):
        for start in range(0, count, step):
            span = pl.ds(first + start, step)
            yield keys[part, span].reshape(tile, HEAD), values[part, span].reshape(tile, HEAD)

    def finish(sums):
        return (sums[:, :HEAD] / sums[:, HEAD:]).astype(BF16)

    @pl.when(safe)
    def _():
        pair = scaled_split(query)
        sums = out_ref if mode == "own" else acc
        sums[...] = acc_in[0][...] if mode == "more" else jnp.zeros_like(sums)

        def half_part(index, carry):
            part = index // 2

            @pl.when(valid_ref[part] > 0)
            def _():
                half = blocks // 2
                for key, value in tiles(part, lax.rem(index, 2) * half, half):
                    sums[...] += weighted(jnp.exp2(score_tile(pair, key)), value)

            return carry

        lax.fori_loop(2 if mode == "more" else 0, 2 * parts, half_part, 0)
        if mode != "own":
            out_ref[...] = finish(sums[...]).reshape(out_ref.shape)

    if mode == "own":
        return

    @pl.when(jnp.logical_not(safe))
    def _():
        def one_block(block, carry):
            pair = scaled_split(query_ref[block])
            sums = acc.at[pl.ds(0, rows)]
            sums[...] = jnp.zeros_like(sums)
            top[...] = jnp.full_like(top, LOWEST)

            def one_part(part, carry):
                @pl.when(valid_ref[part] > 0)
                def _():
                    for key, value in tiles(part):
                        scores = score_tile(pair, key)
                        old_top = top[:, :1]
                        new_top = jnp.maximum(old_top, jnp.max(scores, axis=1, keepdims=True))
                        part_sums = weighted(jnp.exp2(scores - new_top), value)
                        sums[...] = sums[...] * jnp.exp2(old_top - new_top) + part_sums
                        top[...] = jnp.broadcast_to(new_top, top.shape)

                return carry

            lax.fori_loop(0, parts, one_part, 0)
            out_ref[block] = finish(sums[...])
            return carry

        lax.fori_loop(0, blocks, one_block, 0)


def whole(array):
    return pl.BlockSpec(
        array.shape, lambda i: (0,) * len(array.shape), pipeline_mode=pl.Buffered(1)
    )


ANY = pl.BlockSpec(memory_space=pl.ANY)
SMEM = pl.BlockSpec(memory_space=pltpu.SMEM)


def attend(mode, frame, valid, query, key, value, key_extra=(), value_extra=(), acc=None, tile=512):
    blocks, rows, _ = query.shape
    total = blocks * rows
    parts = valid.shape[0] if mode != "own" else 1
    pieces = len(key_extra)
    if mode == "own":
        out = jax.ShapeDtypeStruct((total, 2 * HEAD), F32)
    else:
        out = jax.ShapeDtypeStruct((blocks, rows, HEAD), BF16)
    accs = [acc] if mode == "more" else []
    return pl.pallas_call(
        functools.partial(attend_kernel, frame=frame, tile=tile, pieces=pieces, mode=mode),
        grid=(1,),
        in_specs=[SMEM, whole(query), ANY, ANY, *[ANY] * (2 * pieces), *[whole(a) for a in accs]],
        out_specs=whole(out),
        out_shape=out,
        scratch_shapes=[
            pltpu.VMEM((parts, blocks, rows, HEAD), BF16),
            pltpu.VMEM((parts, blocks, rows, HEAD), BF16),
            pltpu.VMEM((total, 2 * HEAD), F32),
            pltpu.VMEM((rows, HEAD), F32),
            pltpu.SemaphoreType.DMA((parts, max(1, pieces))),
            pltpu.SemaphoreType.DMA((parts, max(1, pieces))),
        ],
        compiler_params=pltpu.CompilerParams(vmem_limit_bytes=24 << 20),
        cost_estimate=pl.CostEstimate(
            flops=4 * total * total * HEAD * (parts - (mode == "more")),
            bytes_accessed=4 * total * HEAD * (1 + parts),
            transcendentals=total * total,
        ),
    )(valid, query, key, value, *key_extra, *value_extra, *accs)


def cut_kernel(place_ref, keyframes_ref, source_ref, *refs, xs):
    *out_refs, sem = refs
    blocks, frames = source_ref.shape[:2]
    quarter = blocks // xs
    x = place_ref[0] // 2
    copies = []
    for step, out_ref in enumerate(out_refs, 1):
        start = lax.rem(x + step, xs) * quarter
        for j in range(out_ref.shape[0]):
            slot = lax.rem(keyframes_ref[j], frames)
            copies.append(
                pltpu.make_async_copy(
                    source_ref.at[pl.ds(start, quarter), slot], out_ref.at[j], sem.at[len(copies)]
                )
            )
    for copy in copies:
        copy.start()
    for copy in copies:
        copy.wait()


def pick_x_kernel(place_ref, keyframes_ref, source_ref, *refs):
    *got_refs, out_ref, sem = refs
    xs = len(got_refs) + 1
    blocks, frames = source_ref.shape[:2]
    quarter = blocks // xs
    x = place_ref[0] // 2
    extras = out_ref.shape[0]
    for j in range(extras):
        keyframe = keyframes_ref[j]
        step = lax.rem(x - keyframe // (2 * frames) + xs, xs)

        @pl.when(step == 0)
        def _():
            slot = lax.rem(keyframe, frames)
            pltpu.make_async_copy(
                source_ref.at[pl.ds(x * quarter, quarter), slot], out_ref.at[j], sem.at[j]
            ).start()

        for which, got_ref in enumerate(got_refs, 1):

            @pl.when(step == which)
            def _():
                pltpu.make_async_copy(got_ref.at[j], out_ref.at[j], sem.at[j]).start()

    for j in range(extras):
        pltpu.make_async_copy(got_refs[0].at[j], out_ref.at[j], sem.at[j]).wait()


def pick_y_kernel(place_ref, keyframes_ref, mine_ref, other_ref, out_ref, sem, *, frames):
    y = lax.rem(place_ref[0], 2)
    extras = out_ref.shape[0]
    for j in range(extras):
        same = lax.rem(keyframes_ref[j] // frames, 2) == y

        @pl.when(same)
        def _():
            pltpu.make_async_copy(mine_ref.at[j], out_ref.at[j], sem.at[j]).start()

        @pl.when(jnp.logical_not(same))
        def _():
            pltpu.make_async_copy(other_ref.at[j], out_ref.at[j], sem.at[j]).start()

    for j in range(extras):
        pltpu.make_async_copy(mine_ref.at[j], out_ref.at[j], sem.at[j]).wait()


def move_call(kernel, out_shapes, place, keyframes, *arrays):
    moved = sum(math.prod(o.shape) for o in out_shapes)
    return pl.pallas_call(
        kernel,
        grid=(1,),
        in_specs=[SMEM, SMEM] + [ANY] * len(arrays),
        out_specs=[whole(o) for o in out_shapes],
        out_shape=out_shapes,
        scratch_shapes=[pltpu.SemaphoreType.DMA((len(out_shapes) * keyframes.shape[0],))],
        compiler_params=pltpu.CompilerParams(vmem_limit_bytes=8 << 20),
        cost_estimate=pl.CostEstimate(flops=0, bytes_accessed=4 * moved, transcendentals=0),
    )(place, keyframes, *arrays)


def piece_shape(keyframes, by_frame, xs):
    blocks, _, rows, width = by_frame.shape
    return jax.ShapeDtypeStruct((keyframes.shape[0], blocks // xs, rows, width), BF16)


def cut_pieces(place, keyframes, by_frame, xs):
    return move_call(
        functools.partial(cut_kernel, xs=xs),
        [piece_shape(keyframes, by_frame, xs)] * (xs - 1), place, keyframes, by_frame,
    )


def pick_along_x(place, keyframes, by_frame, got):
    return move_call(
        pick_x_kernel,
        [piece_shape(keyframes, by_frame, len(got) + 1)], place, keyframes, by_frame, *got,
    )[0]


def pick_along_y(place, keyframes, mine, other, frames):
    return move_call(
        functools.partial(pick_y_kernel, frames=frames),
        [jax.ShapeDtypeStruct(mine.shape, BF16)], place, keyframes, mine, other,
    )[0]


def swap_branch(value):
    return lax.ppermute(value, "branch", [(0, 1), (1, 0)])


def to_heads(value):
    return lax.all_to_all(value, "seq", split_axis=0, concat_axis=0, tiled=True)


def shift_x(value, step):
    size = lax.axis_size("mp")
    return lax.ppermute(value, "mp", [(m, (m + 2 * step) % size) for m in range(size)])


def flip_y(value):
    size = lax.axis_size("mp")
    return lax.ppermute(value, "mp", [(m, m ^ 1) for m in range(size)])


def spread_keyframes(by_frame, keyframes):
    place = lax.axis_index("mp").astype(jnp.int32).reshape(1)
    xs = lax.axis_size("mp") // 2
    pieces = cut_pieces(place, keyframes, by_frame, xs)
    got = [shift_x(piece, step) for step, piece in enumerate(pieces, 1)]
    mine = pick_along_x(place, keyframes, by_frame, got)
    other = flip_y(mine)
    mine = pick_along_y(place, keyframes, mine, other, by_frame.shape[1])
    return [mine] + [shift_x(mine, step) for step in range(1, xs)]


def local(queries, keys, values, inject, keyframes, key_mask):
    queries, keys, values = queries[0], keys[0], values[0]
    frames = queries.shape[0]
    partner_keys = swap_branch(keys)
    partner_queries = swap_branch(queries)

    value_rows = split_heads(values)
    value_heads = to_heads(value_rows)
    value_extra = spread_keyframes(value_heads, keyframes)

    (key_rows,) = blend_heads(inject, keys, partner_keys, False)
    key_heads = to_heads(key_rows)
    key_extra = spread_keyframes(key_heads, keyframes)

    query_rows = blend_heads(inject, queries, partner_queries, True)
    query_frames = []
    for f in range(frames):
        query_frames.append(to_heads(query_rows[f]))

    first = lax.axis_index("mp") * frames
    outs = []
    for f in range(frames):
        masks = lax.dynamic_index_in_dim(key_mask, first + f, 0, keepdims=False)
        valid = jnp.concatenate([jnp.ones((1,), jnp.int32), masks])
        extra = (key_extra, value_extra)
        if f == 0:
            acc = attend("own", f, valid, query_frames[f], key_heads, value_heads)
            out = attend("more", f, valid, query_frames[f], key_heads, value_heads, *extra, acc)
        else:
            out = attend("all", f, valid, query_frames[f], key_heads, value_heads, *extra)
        back = to_heads(out)
        heads, rows, _ = back.shape
        outs.append(back.transpose(1, 0, 2).reshape(rows, heads * HEAD))
    return jnp.stack(outs)[None]


def solution(mesh):
    return jax.shard_map(
        local,
        mesh=mesh,
        in_specs=(
            P("branch", "mp", "seq", None),
            P("branch", "mp", "seq", None),
            P("branch", "mp", "seq", None),
            P("branch", None),
            P(),
            P(),
        ),
        out_specs=P("branch", "mp", "seq", None),
        check_vma=False,
    )
```

```python
import functools
import math

import jax
import jax.numpy as jnp
from jax import lax
from jax.experimental import pallas as pl
from jax.experimental.pallas import tpu as pltpu
from jax.sharding import PartitionSpec as P


HEAD = 128
SCALE = math.log2(math.e) / math.sqrt(HEAD)
SAFE = 100.0
LOWEST = -1e30
BF16 = jnp.bfloat16
F32 = jnp.float32


ANY = pl.BlockSpec(memory_space=pl.ANY)
SMEM = pl.BlockSpec(memory_space=pltpu.SMEM)


def blend_kernel(strength_ref, own_ref, partner_ref, out_ref, *, heads):
    first = pl.program_id(0) * heads
    for head in range(heads):
        share = strength_ref[0, first + head]
        lanes = slice(head * HEAD, (head + 1) * HEAD)
        out_ref[head] = (
            (1.0 - share) * own_ref[:, :, lanes].astype(F32)
            + share * partner_ref[:, :, lanes].astype(F32)
        ).astype(BF16)


def blend_heads(strength, own, partner, steps=2):
    frames, rows, width = own.shape
    heads = width // HEAD
    group = heads // steps
    block = pl.BlockSpec((frames, rows, group * HEAD), lambda h: (0, 0, h))
    return pl.pallas_call(
        functools.partial(blend_kernel, heads=group),
        grid=(steps,),
        in_specs=[SMEM, block, block],
        out_specs=pl.BlockSpec((group, frames, rows, HEAD), lambda h: (h, 0, 0, 0)),
        out_shape=jax.ShapeDtypeStruct((heads, frames, rows, HEAD), BF16),
        cost_estimate=pl.CostEstimate(
            flops=3 * own.size, bytes_accessed=6 * own.size, transcendentals=0
        ),
        name="blend",
    )(strength, own, partner)


def split_kernel(source_ref, out_ref, sem):
    heads = out_ref.shape[0]
    copies = [
        pltpu.make_async_copy(
            source_ref.at[:, :, pl.ds(head * HEAD, HEAD)], out_ref.at[head], sem.at[head]
        )
        for head in range(heads)
    ]
    for copy in copies:
        copy.start()
    for copy in copies:
        copy.wait()


def split_heads(rows):
    frames, count, width = rows.shape
    heads = width // HEAD
    out = jax.ShapeDtypeStruct((heads, frames, count, HEAD), BF16)
    return pl.pallas_call(
        split_kernel,
        grid=(1,),
        in_specs=[ANY],
        out_specs=whole(out),
        out_shape=out,
        scratch_shapes=[pltpu.SemaphoreType.DMA((heads,))],
        cost_estimate=pl.CostEstimate(flops=0, bytes_accessed=4 * rows.size, transcendentals=0),
        name="split_heads",
    )(rows)


def dot_nt(a, b):
    return lax.dot_general(a, b, (((1,), (1,)), ((), ())), preferred_element_type=F32)


def scaled_split(query):
    scaled = query.astype(F32) * SCALE
    high = scaled.astype(BF16)
    low = (scaled - high.astype(F32)).astype(BF16)
    return jnp.concatenate([high, low], axis=1)


def score_tile(query_pair, key):
    return dot_nt(query_pair, jnp.concatenate([key, key], axis=1))


def with_ones(value):
    return jnp.concatenate([value, jnp.ones_like(value)], axis=1)


def weighted(weights, value):
    return jnp.dot(weights.astype(BF16), with_ones(value), preferred_element_type=F32)


def norm_max(rows):
    rows = rows.reshape(-1, HEAD)
    sums = jnp.dot(rows * rows, jnp.ones((HEAD, HEAD), BF16), preferred_element_type=F32)
    return jnp.max(sums)


def attend_kernel(valid_ref, *refs, frame, pieces, mode):
    refs = list(refs)
    frame = pl.program_id(0) if mode == "own" else frame
    unsafe_in, acc_in = (refs.pop(0), refs.pop(0)) if mode == "more" else (None, None)
    query_ref, key_ref, value_ref = refs[:3]
    key_extra, value_extra = refs[3 : 3 + pieces], refs[3 + pieces : 3 + 2 * pieces]
    refs = refs[3 + 2 * pieces :]
    flag = 0
    if mode == "own":
        acc, unsafe = refs[:2]
        flag = frame
        refs = refs[2:]
    else:
        out_ref, acc, unsafe = refs[:3]
        refs = refs[3:]
    keys, values, top, key_sem, value_sem = refs
    parts, cuts = keys.shape[:2]
    blocks, rows = query_ref.shape[-3], query_ref.shape[-2]
    quarter = blocks // cuts
    tile = quarter * rows

    def fetch(part):
        for cut in range(cuts):
            if part == 0:
                span = pl.ds(cut * quarter, quarter)
                key, value = key_ref.at[span, frame], value_ref.at[span, frame]
            else:
                key, value = key_extra[cut].at[part - 1], value_extra[cut].at[part - 1]
            yield (
                pltpu.make_async_copy(key, keys.at[part, cut], key_sem.at[part, cut]),
                pltpu.make_async_copy(value, values.at[part, cut], value_sem.at[part, cut]),
            )

    def start(part):
        for key_copy, value_copy in fetch(part):
            key_copy.start()
            value_copy.start()

    def wait(target, sem, part):
        for cut in range(cuts):
            there = target.at[part, cut]
            pltpu.make_async_copy(there, there, sem.at[part, cut]).wait()

    def rows_of(target, part, cut):
        return target[part, cut].reshape(tile, HEAD)

    def add_part(part, pair, query_norm, assign):
        wait(keys, key_sem, part)
        safe = query_norm * norm_max(keys[part]) * (SCALE * SCALE) <= SAFE * SAFE
        wait(values, value_sem, part)

        @pl.when(safe)
        def _():
            for cut in range(cuts):
                weights = jnp.exp2(score_tile(pair, rows_of(keys, part, cut)))
                sums = weighted(weights, rows_of(values, part, cut))
                acc[...] = sums if assign and cut == 0 else acc[...] + sums

        @pl.when(jnp.logical_not(safe))
        def _():
            unsafe[flag] = 1

    first = 1 if mode == "more" else 0
    if first == 0:
        start(0)
    for part in range(1, parts):

        @pl.when(valid_ref[part] > 0)
        def _():
            start(part)

    query = query_ref[...].reshape(-1, HEAD)
    query_norm = norm_max(query)
    pair = scaled_split(query)
    if mode == "more":
        unsafe[0] = unsafe_in[frame]
        acc[...] = acc_in[...]
    else:
        unsafe[flag] = 0
        add_part(0, pair, query_norm, True)

    if mode == "own":
        return

    def one_part(part, carry):
        @pl.when(valid_ref[part] > 0)
        def _():
            add_part(part, pair, query_norm, False)

        return carry

    lax.fori_loop(1, parts, one_part, 0)

    def finish(sums):
        return (sums[:, :HEAD] / sums[:, HEAD:]).astype(BF16)

    @pl.when(unsafe[0] == 0)
    def _():
        out_ref[...] = finish(acc[...]).reshape(out_ref.shape)

    @pl.when(unsafe[0] > 0)
    def _():
        if mode == "more":
            start(0)
            wait(keys, key_sem, 0)
            wait(values, value_sem, 0)

        def one_block(block, carry):
            pair = scaled_split(query_ref[block])
            sums = acc.at[pl.ds(0, rows)]
            sums[...] = jnp.zeros_like(sums)
            top[...] = jnp.full_like(top, LOWEST)

            def slow_part(part, carry):
                @pl.when(valid_ref[part] > 0)
                def _():
                    for cut in range(cuts):
                        scores = score_tile(pair, rows_of(keys, part, cut))
                        old_top = top[:, :1]
                        new_top = jnp.maximum(old_top, jnp.max(scores, axis=1, keepdims=True))
                        part_sums = weighted(
                            jnp.exp2(scores - new_top), rows_of(values, part, cut)
                        )
                        sums[...] = sums[...] * jnp.exp2(old_top - new_top) + part_sums
                        top[...] = jnp.broadcast_to(new_top, top.shape)

                return carry

            lax.fori_loop(0, parts, slow_part, 0)
            out_ref[block] = finish(sums[...])
            return carry

        lax.fori_loop(0, blocks, one_block, 0)


def whole(array):
    return pl.BlockSpec(
        array.shape, lambda i: (0,) * len(array.shape), pipeline_mode=pl.Buffered(1)
    )


def attend(mode, frame, valid, query, key, value, key_extra=(), value_extra=(), own=(), cuts=4):
    blocks, frames, rows, _ = query.shape
    total = blocks * rows
    parts = valid.shape[0] if mode != "own" else 1
    pieces = len(key_extra)
    acc = jax.ShapeDtypeStruct((frames, total, 2 * HEAD), F32)
    flag = jax.ShapeDtypeStruct((frames,), jnp.int32)
    out = jax.ShapeDtypeStruct((blocks, rows, HEAD), BF16)
    kept = pltpu.VMEM((parts, cuts, blocks // cuts, rows, HEAD), BF16)
    sems = pltpu.SemaphoreType.DMA((parts, cuts))
    scratch = [kept, kept, pltpu.VMEM((rows, HEAD), F32), sems, sems]
    if mode == "own":
        out_shape = [acc, flag]
        out_specs = [pl.BlockSpec((None, total, 2 * HEAD), lambda i: (i, 0, 0)), SMEM]
    else:
        out_shape, out_specs = [out], [whole(out)]
        scratch = [pltpu.VMEM(acc.shape[1:], F32), pltpu.SMEM((1,), jnp.int32)] + scratch
    if mode == "own":
        query_spec = pl.BlockSpec((blocks, None, rows, HEAD), lambda i: (0, i, 0, 0))
    else:
        query_spec = pl.BlockSpec(
            (blocks, None, rows, HEAD), lambda i: (0, frame, 0, 0), pipeline_mode=pl.Buffered(1)
        )
    acc_spec = pl.BlockSpec(
        (None, total, 2 * HEAD), lambda i: (frame, 0, 0), pipeline_mode=pl.Buffered(1)
    )
    result = pl.pallas_call(
        functools.partial(attend_kernel, frame=frame, pieces=pieces, mode=mode),
        grid=(frames if mode == "own" else 1,),
        in_specs=[
            SMEM,
            *([SMEM, acc_spec] if own else []),
            query_spec,
            *[ANY] * (2 + 2 * pieces),
        ],
        out_specs=out_specs,
        out_shape=out_shape,
        scratch_shapes=scratch,
        compiler_params=pltpu.CompilerParams(vmem_limit_bytes=24 << 20),
        cost_estimate=pl.CostEstimate(
            flops=8 * total * total * HEAD,
            bytes_accessed=4 * total * HEAD * (1 + parts),
            transcendentals=2 * total * total,
        ),
    )(valid, *own[::-1], query, key, value, *key_extra, *value_extra)
    return result if mode == "own" else result[0]


def cut_kernel(place_ref, keyframes_ref, source_ref, *refs, xs):
    *out_refs, sem = refs
    blocks, frames = source_ref.shape[:2]
    quarter = blocks // xs
    x = place_ref[0] // 2
    copies = []
    for step, out_ref in enumerate(out_refs, 1):
        start = lax.rem(x + step, xs) * quarter
        for j in range(out_ref.shape[0]):
            slot = lax.rem(keyframes_ref[j], frames)
            copies.append(
                pltpu.make_async_copy(
                    source_ref.at[pl.ds(start, quarter), slot], out_ref.at[j], sem.at[len(copies)]
                )
            )
    for copy in copies:
        copy.start()
    for copy in copies:
        copy.wait()


def pick_x_kernel(place_ref, keyframes_ref, source_ref, *refs):
    *got_refs, out_ref, sem = refs
    xs = len(got_refs) + 1
    blocks, frames = source_ref.shape[:2]
    quarter = blocks // xs
    x = place_ref[0] // 2
    extras = out_ref.shape[0]
    for j in range(extras):
        keyframe = keyframes_ref[j]
        step = lax.rem(x - keyframe // (2 * frames) + xs, xs)

        @pl.when(step == 0)
        def _():
            slot = lax.rem(keyframe, frames)
            pltpu.make_async_copy(
                source_ref.at[pl.ds(x * quarter, quarter), slot], out_ref.at[j], sem.at[j]
            ).start()

        for which, got_ref in enumerate(got_refs, 1):

            @pl.when(step == which)
            def _():
                pltpu.make_async_copy(got_ref.at[j], out_ref.at[j], sem.at[j]).start()

    for j in range(extras):
        pltpu.make_async_copy(got_refs[0].at[j], out_ref.at[j], sem.at[j]).wait()


def pick_y_kernel(place_ref, keyframes_ref, mine_ref, other_ref, out_ref, sem, *, frames):
    y = lax.rem(place_ref[0], 2)
    extras = out_ref.shape[0]
    for j in range(extras):
        same = lax.rem(keyframes_ref[j] // frames, 2) == y

        @pl.when(same)
        def _():
            pltpu.make_async_copy(mine_ref.at[j], out_ref.at[j], sem.at[j]).start()

        @pl.when(jnp.logical_not(same))
        def _():
            pltpu.make_async_copy(other_ref.at[j], out_ref.at[j], sem.at[j]).start()

    for j in range(extras):
        pltpu.make_async_copy(mine_ref.at[j], out_ref.at[j], sem.at[j]).wait()


def move_call(kernel, out_shapes, place, keyframes, *arrays):
    moved = sum(math.prod(o.shape) for o in out_shapes)
    return pl.pallas_call(
        kernel,
        grid=(1,),
        in_specs=[SMEM, SMEM] + [ANY] * len(arrays),
        out_specs=[whole(o) for o in out_shapes],
        out_shape=out_shapes,
        scratch_shapes=[pltpu.SemaphoreType.DMA((len(out_shapes) * keyframes.shape[0],))],
        compiler_params=pltpu.CompilerParams(vmem_limit_bytes=8 << 20),
        cost_estimate=pl.CostEstimate(flops=0, bytes_accessed=4 * moved, transcendentals=0),
    )(place, keyframes, *arrays)


def piece_shape(keyframes, by_frame, xs):
    blocks, _, rows, width = by_frame.shape
    return jax.ShapeDtypeStruct((keyframes.shape[0], blocks // xs, rows, width), BF16)


def cut_pieces(place, keyframes, by_frame, xs):
    return move_call(
        functools.partial(cut_kernel, xs=xs),
        [piece_shape(keyframes, by_frame, xs)] * (xs - 1), place, keyframes, by_frame,
    )


def pick_along_x(place, keyframes, by_frame, got):
    return move_call(
        pick_x_kernel,
        [piece_shape(keyframes, by_frame, len(got) + 1)], place, keyframes, by_frame, *got,
    )[0]


def pick_along_y(place, keyframes, mine, other, frames):
    return move_call(
        functools.partial(pick_y_kernel, frames=frames),
        [jax.ShapeDtypeStruct(mine.shape, BF16)], place, keyframes, mine, other,
    )[0]


def swap_branch(value):
    return lax.ppermute(value, "branch", [(0, 1), (1, 0)])


def to_heads(value):
    return lax.all_to_all(value, "seq", split_axis=0, concat_axis=0, tiled=True)


def shift_x(value, step):
    size = lax.axis_size("mp")
    return lax.ppermute(value, "mp", [(m, (m + 2 * step) % size) for m in range(size)])


def flip_y(value):
    size = lax.axis_size("mp")
    return lax.ppermute(value, "mp", [(m, m ^ 1) for m in range(size)])


def spread_keyframes(by_frame, keyframes):
    place = lax.axis_index("mp").astype(jnp.int32).reshape(1)
    xs = lax.axis_size("mp") // 2
    pieces = cut_pieces(place, keyframes, by_frame, xs)
    got = [shift_x(piece, step) for step, piece in enumerate(pieces, 1)]
    mine = pick_along_x(place, keyframes, by_frame, got)
    other = flip_y(mine)
    mine = pick_along_y(place, keyframes, mine, other, by_frame.shape[1])
    return [mine] + [shift_x(mine, step) for step in range(1, xs)]


def local(queries, keys, values, inject, keyframes, key_mask):
    queries, keys, values = queries[0], keys[0], values[0]
    frames = queries.shape[0]
    partner_keys = swap_branch(keys)
    partner_queries = swap_branch(queries)

    value_rows = split_heads(values)
    value_heads = to_heads(value_rows)
    value_extra = spread_keyframes(value_heads, keyframes)

    key_rows = blend_heads(inject, keys, partner_keys)
    key_heads = to_heads(key_rows)
    key_extra = spread_keyframes(key_heads, keyframes)

    query_rows = blend_heads(inject, queries, partner_queries)
    query_heads = to_heads(query_rows)

    first = lax.axis_index("mp") * frames
    always = jnp.ones((1,), jnp.int32)
    own = attend("own", None, always, query_heads, key_heads, value_heads)
    outs = []
    for f in range(frames):
        masks = lax.dynamic_index_in_dim(key_mask, first + f, 0, keepdims=False)
        valid = jnp.concatenate([always, masks])
        out = attend(
            "more", f, valid, query_heads, key_heads, value_heads,
            key_extra, value_extra, own,
        )
        back = to_heads(out)
        heads, rows, _ = back.shape
        outs.append(back.transpose(1, 0, 2).reshape(rows, heads * HEAD))
    return jnp.stack(outs)[None]


def solution(mesh):
    return jax.shard_map(
        local,
        mesh=mesh,
        in_specs=(
            P("branch", "mp", "seq", None),
            P("branch", "mp", "seq", None),
            P("branch", "mp", "seq", None),
            P("branch", None),
            P(),
            P(),
        ),
        out_specs=P("branch", "mp", "seq", None),
        check_vma=False,
    )
```

```python
import functools
import math

import jax
import jax.numpy as jnp
from jax import lax
from jax.experimental import pallas as pl
from jax.experimental.pallas import tpu as pltpu
from jax.sharding import PartitionSpec as P


HEAD = 128
SCALE = math.log2(math.e) / math.sqrt(HEAD)
SAFE = 100.0
LOWEST = -1e30
BF16 = jnp.bfloat16
F32 = jnp.float32


ANY = pl.BlockSpec(memory_space=pl.ANY)
SMEM = pl.BlockSpec(memory_space=pltpu.SMEM)


def blend_kernel(strength_ref, own_ref, partner_ref, *out_refs, heads):
    first = pl.program_id(0) * heads
    for head in range(heads):
        share = strength_ref[0, first + head]
        lanes = slice(head * HEAD, (head + 1) * HEAD)
        mixed = (
            (1.0 - share) * own_ref[:, :, lanes].astype(F32)
            + share * partner_ref[:, :, lanes].astype(F32)
        ).astype(BF16)
        if len(out_refs) == 1:
            out_refs[0][head] = mixed.reshape(-1, HEAD)
        else:
            for frame, out_ref in enumerate(out_refs):
                out_ref[head] = mixed[frame]


def blend_heads(strength, own, partner, split, steps=2):
    frames, rows, width = own.shape
    heads = width // HEAD
    group = heads // steps
    outs, count = (frames, rows) if split else (1, frames * rows)
    block = pl.BlockSpec((frames, rows, group * HEAD), lambda h: (0, 0, h))
    return pl.pallas_call(
        functools.partial(blend_kernel, heads=group),
        grid=(steps,),
        in_specs=[SMEM, block, block],
        out_specs=[pl.BlockSpec((group, count, HEAD), lambda h: (h, 0, 0))] * outs,
        out_shape=[jax.ShapeDtypeStruct((heads, count, HEAD), BF16)] * outs,
        cost_estimate=pl.CostEstimate(
            flops=3 * own.size, bytes_accessed=6 * own.size, transcendentals=0
        ),
        name="blend",
    )(strength, own, partner)


def split_kernel(source_ref, out_ref, sem):
    heads = out_ref.shape[0]
    copies = [
        pltpu.make_async_copy(
            source_ref.at[:, :, pl.ds(head * HEAD, HEAD)], out_ref.at[head], sem.at[head]
        )
        for head in range(heads)
    ]
    for copy in copies:
        copy.start()
    for copy in copies:
        copy.wait()


def split_heads(rows):
    frames, count, width = rows.shape
    heads = width // HEAD
    out = jax.ShapeDtypeStruct((heads, frames, count, HEAD), BF16)
    return pl.pallas_call(
        split_kernel,
        grid=(1,),
        in_specs=[ANY],
        out_specs=whole(out),
        out_shape=out,
        scratch_shapes=[pltpu.SemaphoreType.DMA((heads,))],
        cost_estimate=pl.CostEstimate(flops=0, bytes_accessed=4 * rows.size, transcendentals=0),
        name="split_heads",
    )(rows)


def dot_nt(a, b):
    return lax.dot_general(a, b, (((1,), (1,)), ((), ())), preferred_element_type=F32)


def scaled_split(query):
    scaled = query.astype(F32) * SCALE
    high = scaled.astype(BF16)
    low = (scaled - high.astype(F32)).astype(BF16)
    return jnp.concatenate([high, low], axis=1)


def score_tile(query_pair, key):
    return dot_nt(query_pair, jnp.concatenate([key, key], axis=1))


def with_ones(value):
    return jnp.concatenate([value, jnp.ones_like(value)], axis=1)


def weighted(weights, value):
    return jnp.dot(weights.astype(BF16), with_ones(value), preferred_element_type=F32)


def norm_max(rows):
    rows = rows.reshape(-1, HEAD)
    sums = jnp.dot(rows * rows, jnp.ones((HEAD, HEAD), BF16), preferred_element_type=F32)
    return jnp.max(sums)


def attend_kernel(valid_ref, *refs, frame, pieces, rows, mode):
    refs = list(refs)
    unsafe_in, acc_in = (refs.pop(0), refs.pop(0)) if mode == "more" else (None, None)
    query_in, key_ref, value_ref = refs[:3]
    key_extra, value_extra = refs[3 : 3 + pieces], refs[3 + pieces : 3 + 2 * pieces]
    refs = refs[3 + 2 * pieces :]
    if mode != "own":
        out_ref = refs.pop(0)
    acc, unsafe, keys, values, query_ref, top, key_sem, value_sem, sem = refs
    parts, cuts, blocks, cut_rows = keys.shape[:4]
    tile = blocks * cut_rows

    def fetch(part):
        for cut in range(cuts):
            if part == 0:
                span = pl.ds(frame * rows + cut * cut_rows, cut_rows)
                key, value = key_ref.at[:, span], value_ref.at[:, span]
            else:
                key, value = key_extra[cut].at[part - 1], value_extra[cut].at[part - 1]
            yield (
                pltpu.make_async_copy(key, keys.at[part, cut], key_sem.at[part, cut]),
                pltpu.make_async_copy(value, values.at[part, cut], value_sem.at[part, cut]),
            )

    def start(part):
        for key_copy, value_copy in fetch(part):
            key_copy.start()
            value_copy.start()

    def wait(target, sem, part):
        for cut in range(cuts):
            there = target.at[part, cut]
            pltpu.make_async_copy(there, there, sem.at[part, cut]).wait()

    def rows_of(target, part, cut):
        return target[part, cut].reshape(tile, HEAD)

    def add_part(part, pair, query_norm, assign):
        wait(keys, key_sem, part)
        safe = query_norm * norm_max(keys[part]) * (SCALE * SCALE) <= SAFE * SAFE
        wait(values, value_sem, part)

        @pl.when(safe)
        def _():
            for cut in range(cuts):
                weights = jnp.exp2(score_tile(pair, rows_of(keys, part, cut)))
                sums = weighted(weights, rows_of(values, part, cut))
                acc[...] = sums if assign and cut == 0 else acc[...] + sums

        @pl.when(jnp.logical_not(safe))
        def _():
            unsafe[0] = 1

    query_copy = pltpu.make_async_copy(query_in, query_ref, sem.at[0])
    query_copy.start()
    if mode == "more":
        acc_copy = pltpu.make_async_copy(acc_in, acc, sem.at[1])
        acc_copy.start()
    else:
        start(0)
    for part in range(1, parts):

        @pl.when(valid_ref[part] > 0)
        def _():
            start(part)

    query_copy.wait()
    query = query_ref[...].reshape(-1, HEAD)
    query_norm = norm_max(query)
    pair = scaled_split(query)
    if mode == "more":
        unsafe[0] = unsafe_in[0]
        acc_copy.wait()
    else:
        unsafe[0] = 0

    if mode == "own":
        add_part(0, pair, query_norm, True)
        return
    if mode == "all":
        acc[...] = jnp.zeros_like(acc)

    def one_part(part, carry):
        @pl.when(valid_ref[part] > 0)
        def _():
            add_part(part, pair, query_norm, False)

        return carry

    lax.fori_loop(1 if mode == "more" else 0, parts, one_part, 0)

    def finish(sums):
        return (sums[:, :HEAD] / sums[:, HEAD:]).astype(BF16)

    @pl.when(unsafe[0] == 0)
    def _():
        out_ref[...] = finish(acc[...]).reshape(out_ref.shape)

    @pl.when(unsafe[0] > 0)
    def _():
        if mode == "more":
            start(0)
            wait(keys, key_sem, 0)
            wait(values, value_sem, 0)

        def one_block(block, carry):
            pair = scaled_split(query_ref[block])
            sums = acc.at[pl.ds(0, rows)]
            sums[...] = jnp.zeros_like(sums)
            top[...] = jnp.full_like(top, LOWEST)

            def slow_part(part, carry):
                @pl.when(valid_ref[part] > 0)
                def _():
                    for cut in range(cuts):
                        scores = score_tile(pair, rows_of(keys, part, cut))
                        old_top = top[:, :1]
                        new_top = jnp.maximum(old_top, jnp.max(scores, axis=1, keepdims=True))
                        part_sums = weighted(
                            jnp.exp2(scores - new_top), rows_of(values, part, cut)
                        )
                        sums[...] = sums[...] * jnp.exp2(old_top - new_top) + part_sums
                        top[...] = jnp.broadcast_to(new_top, top.shape)

                return carry

            lax.fori_loop(0, parts, slow_part, 0)
            out_ref[block] = finish(sums[...])
            return carry

        lax.fori_loop(0, query_ref.shape[0], one_block, 0)


def whole(array):
    return pl.BlockSpec(
        array.shape, lambda i: (0,) * len(array.shape), pipeline_mode=pl.Buffered(1)
    )


def attend(mode, frame, valid, query, key, value, key_extra=(), value_extra=(), own=(), cuts=4):
    blocks, rows, _ = query.shape
    total = blocks * rows
    parts = valid.shape[0]
    pieces = len(key_extra)
    acc = jax.ShapeDtypeStruct((total, 2 * HEAD), F32)
    flag = jax.ShapeDtypeStruct((1,), jnp.int32)
    out = jax.ShapeDtypeStruct((blocks, rows, HEAD), BF16)
    kept = pltpu.VMEM((parts, cuts, blocks, rows // cuts, HEAD), BF16)
    sems = pltpu.SemaphoreType.DMA((parts, cuts))
    scratch = [
        kept, kept, pltpu.VMEM(query.shape, BF16), pltpu.VMEM((rows, HEAD), F32),
        sems, sems, pltpu.SemaphoreType.DMA((2,)),
    ]
    if mode == "own":
        out_shape, out_specs = [acc, flag], [whole(acc), SMEM]
    else:
        out_shape, out_specs = [out], [whole(out)]
        scratch = [pltpu.VMEM(acc.shape, F32), pltpu.SMEM((1,), jnp.int32)] + scratch
    work = {"own": 1, "more": parts - 1, "all": parts}[mode] * total * total
    result = pl.pallas_call(
        functools.partial(attend_kernel, frame=frame, pieces=pieces, rows=rows, mode=mode),
        grid=(1,),
        in_specs=[SMEM, *([SMEM, ANY] if own else []), *[ANY] * (3 + 2 * pieces)],
        out_specs=out_specs,
        out_shape=out_shape,
        scratch_shapes=scratch,
        compiler_params=pltpu.CompilerParams(vmem_limit_bytes=24 << 20),
        cost_estimate=pl.CostEstimate(
            flops=4 * work * HEAD, bytes_accessed=16 * total * HEAD, transcendentals=work
        ),
    )(valid, *own[::-1], query, key, value, *key_extra, *value_extra)
    return result if mode == "own" else result[0]


def piece_rows(keyframe, piece, shape):
    frames, rows, cuts = shape
    start = lax.rem(keyframe, frames) * rows + piece * (rows // cuts)
    return pl.ds(pl.multiple_of(start, rows // cuts), rows // cuts)


def run_copies(copies):
    for copy in copies:
        copy.start()
    for copy in copies:
        copy.wait()


def cut_kernel(place_ref, keyframes_ref, source_ref, *refs, shape):
    *out_refs, sem = refs
    x = place_ref[0] // 2
    copies = []
    for step, out_ref in enumerate(out_refs, 1):
        for j in range(out_ref.shape[0]):
            rows = piece_rows(keyframes_ref[j], lax.rem(x + step, shape[2]), shape)
            copies.append(
                pltpu.make_async_copy(source_ref.at[:, rows], out_ref.at[j], sem.at[len(copies)])
            )
    run_copies(copies)


def pick_x_kernel(place_ref, keyframes_ref, source_ref, *refs, shape, join):
    *got_refs, out_ref, sem = refs
    x = place_ref[0] // 2
    extras, _, cut_rows = got_refs[0].shape[:3]
    kept = source_ref.shape[1]
    if join:
        targets = [out_ref.at[:, pl.ds(kept + j * cut_rows, cut_rows)] for j in range(extras)]
        all_rows = pltpu.make_async_copy(source_ref, out_ref.at[:, pl.ds(0, kept)], sem.at[extras])
        all_rows.start()
    else:
        targets = [out_ref.at[j] for j in range(extras)]
    for j in range(extras):
        keyframe = keyframes_ref[j]
        step = lax.rem(x - keyframe // (2 * shape[0]) + shape[2], shape[2])

        @pl.when(step == 0)
        def _():
            rows = piece_rows(keyframe, x, shape)
            pltpu.make_async_copy(source_ref.at[:, rows], targets[j], sem.at[j]).start()

        for which, got_ref in enumerate(got_refs, 1):

            @pl.when(step == which)
            def _():
                pltpu.make_async_copy(got_ref.at[j], targets[j], sem.at[j]).start()

    for j in range(extras):
        pltpu.make_async_copy(got_refs[0].at[j], targets[j], sem.at[j]).wait()
    if join:
        all_rows.wait()


def pick_y_kernel(place_ref, keyframes_ref, mine_ref, other_ref, out_ref, sem, *, shape, kept):
    y = lax.rem(place_ref[0], 2)
    extras, _, cut_rows = out_ref.shape[:3]
    for j in range(extras):
        if kept is None:
            mine, other = mine_ref.at[j], other_ref.at[j]
        else:
            mine = mine_ref.at[:, pl.ds(kept + j * cut_rows, cut_rows)]
            other = other_ref.at[:, pl.ds(j * cut_rows, cut_rows)]
        same = lax.rem(keyframes_ref[j] // shape[0], 2) == y

        @pl.when(same)
        def _():
            pltpu.make_async_copy(mine, out_ref.at[j], sem.at[j]).start()

        @pl.when(jnp.logical_not(same))
        def _():
            pltpu.make_async_copy(other, out_ref.at[j], sem.at[j]).start()

    for j in range(extras):
        pltpu.make_async_copy(out_ref.at[j], out_ref.at[j], sem.at[j]).wait()


def move_call(kernel, out_shapes, place, keyframes, *arrays):
    moved = sum(math.prod(o.shape) for o in out_shapes)
    return pl.pallas_call(
        kernel,
        grid=(1,),
        in_specs=[SMEM, SMEM] + [ANY] * len(arrays),
        out_specs=[whole(o) for o in out_shapes],
        out_shape=out_shapes,
        scratch_shapes=[pltpu.SemaphoreType.DMA((len(out_shapes) * keyframes.shape[0] + 1,))],
        compiler_params=pltpu.CompilerParams(vmem_limit_bytes=8 << 20),
        cost_estimate=pl.CostEstimate(flops=0, bytes_accessed=4 * moved, transcendentals=0),
    )(place, keyframes, *arrays)


def swap_branch(value):
    return lax.ppermute(value, "branch", [(0, 1), (1, 0)])


def to_heads(value):
    return lax.all_to_all(value, "seq", split_axis=0, concat_axis=0, tiled=True)


def shift_x(value, step):
    size = lax.axis_size("mp")
    return lax.ppermute(value, "mp", [(m, (m + 2 * step) % size) for m in range(size)])


def flip_y(value):
    size = lax.axis_size("mp")
    return lax.ppermute(value, "mp", [(m, m ^ 1) for m in range(size)])


def spread_along_x(place, keyframes, source, shape, join):
    blocks = source.shape[0]
    extras, cut_rows = keyframes.shape[0], shape[1] // shape[2]
    piece = jax.ShapeDtypeStruct((extras, blocks, cut_rows, HEAD), BF16)
    cuts = move_call(
        functools.partial(cut_kernel, shape=shape),
        [piece] * (shape[2] - 1), place, keyframes, source,
    )
    got = [shift_x(cut, step) for step, cut in enumerate(cuts, 1)]
    if join:
        piece = jax.ShapeDtypeStruct((blocks, source.shape[1] + extras * cut_rows, HEAD), BF16)
    return move_call(
        functools.partial(pick_x_kernel, shape=shape, join=join),
        [piece], place, keyframes, source, *got,
    )[0]


def spread_from_x(place, keyframes, mine, shape, kept):
    extras, cut_rows = keyframes.shape[0], shape[1] // shape[2]
    other = flip_y(mine if kept is None else mine[:, kept:])
    blocks = mine.shape[1] if kept is None else mine.shape[0]
    (mine,) = move_call(
        functools.partial(pick_y_kernel, shape=shape, kept=kept),
        [jax.ShapeDtypeStruct((extras, blocks, cut_rows, HEAD), BF16)], place, keyframes, mine, other,
    )
    return [mine] + [shift_x(mine, step) for step in range(1, shape[2])]


def local(queries, keys, values, inject, keyframes, key_mask):
    queries, keys, values = queries[0], keys[0], values[0]
    frames, rows, _ = queries.shape
    shape = (frames, rows, lax.axis_size("mp") // 2)
    place = lax.axis_index("mp").astype(jnp.int32).reshape(1)
    partner_keys = swap_branch(keys)
    partner_queries = swap_branch(queries)

    value_rows = split_heads(values).reshape(-1, frames * rows, HEAD)
    value_heads = to_heads(value_rows)
    value_mine = spread_along_x(place, keyframes, value_heads, shape, False)
    value_extra = spread_from_x(place, keyframes, value_mine, shape, None)

    (key_rows,) = blend_heads(inject, keys, partner_keys, False)
    key_rows = spread_along_x(place, keyframes, key_rows, shape, True)
    key_heads = to_heads(key_rows)
    key_extra = spread_from_x(place, keyframes, key_heads, shape, frames * rows)

    query_rows = blend_heads(inject, queries, partner_queries, True)
    outs = []
    always = jnp.ones((1,), jnp.int32)
    for f in range(frames):
        query = to_heads(query_rows[f])
        masks = lax.dynamic_index_in_dim(key_mask, place[0] * frames + f, 0, keepdims=False)
        valid = jnp.concatenate([always, masks])
        extra = (key_extra, value_extra)
        if f == 0:
            own = attend("own", f, always, query, key_heads, value_heads)
            out = attend("more", f, valid, query, key_heads, value_heads, *extra, own)
        else:
            out = attend("all", f, valid, query, key_heads, value_heads, *extra)
        back = to_heads(out)
        outs.append(back.transpose(1, 0, 2).reshape(rows, -1))
    return jnp.stack(outs)[None]


def solution(mesh):
    return jax.shard_map(
        local,
        mesh=mesh,
        in_specs=(
            P("branch", "mp", "seq", None),
            P("branch", "mp", "seq", None),
            P("branch", "mp", "seq", None),
            P("branch", None),
            P(),
            P(),
        ),
        out_specs=P("branch", "mp", "seq", None),
        check_vma=False,
    )
```

```python
import functools
import math

import jax
import jax.numpy as jnp
from jax import lax
from jax.experimental import pallas as pl
from jax.experimental.pallas import tpu as pltpu
from jax.sharding import PartitionSpec as P


HEAD = 128
SCALE = math.log2(math.e) / math.sqrt(HEAD)
SAFE = 100.0
LOWEST = -1e30
BF16 = jnp.bfloat16
F32 = jnp.float32


ANY = pl.BlockSpec(memory_space=pl.ANY)
SMEM = pl.BlockSpec(memory_space=pltpu.SMEM)


def blend_kernel(strength_ref, own_ref, partner_ref, out_ref, *, heads):
    first = pl.program_id(0) * heads
    for head in range(heads):
        share = strength_ref[0, first + head]
        lanes = slice(head * HEAD, (head + 1) * HEAD)
        mixed = (1.0 - share) * own_ref[:, :, lanes].astype(F32) + share * partner_ref[
            :, :, lanes
        ].astype(F32)
        out_ref[head] = mixed.astype(BF16).reshape(-1, HEAD)


def blend_heads(strength, own, partner, steps=2):
    frames, rows, width = own.shape
    heads = width // HEAD
    group = heads // steps
    block = pl.BlockSpec((frames, rows, group * HEAD), lambda h: (0, 0, h))
    return pl.pallas_call(
        functools.partial(blend_kernel, heads=group),
        grid=(steps,),
        in_specs=[SMEM, block, block],
        out_specs=pl.BlockSpec((group, frames * rows, HEAD), lambda h: (h, 0, 0)),
        out_shape=jax.ShapeDtypeStruct((heads, frames * rows, HEAD), BF16),
        cost_estimate=pl.CostEstimate(
            flops=3 * own.size, bytes_accessed=6 * own.size, transcendentals=0
        ),
        name="blend",
    )(strength, own, partner)


def split_kernel(source_ref, out_ref, sem):
    heads = out_ref.shape[0]
    copies = [
        pltpu.make_async_copy(
            source_ref.at[:, :, pl.ds(head * HEAD, HEAD)], out_ref.at[head], sem.at[head]
        )
        for head in range(heads)
    ]
    for copy in copies:
        copy.start()
    for copy in copies:
        copy.wait()


def split_heads(rows):
    frames, count, width = rows.shape
    heads = width // HEAD
    out = jax.ShapeDtypeStruct((heads, frames, count, HEAD), BF16)
    return pl.pallas_call(
        split_kernel,
        grid=(1,),
        in_specs=[ANY],
        out_specs=whole(out),
        out_shape=out,
        scratch_shapes=[pltpu.SemaphoreType.DMA((heads,))],
        cost_estimate=pl.CostEstimate(flops=0, bytes_accessed=4 * rows.size, transcendentals=0),
        name="split_heads",
    )(rows)


def dot_nt(a, b):
    return lax.dot_general(a, b, (((1,), (1,)), ((), ())), preferred_element_type=F32)


def scaled_split(query):
    scaled = query.astype(F32) * SCALE
    high = scaled.astype(BF16)
    low = (scaled - high.astype(F32)).astype(BF16)
    return jnp.concatenate([high, low], axis=1)


def score_tile(query_pair, key):
    return dot_nt(query_pair, jnp.concatenate([key, key], axis=1))


def with_ones(value):
    return jnp.concatenate([value, jnp.ones_like(value)], axis=1)


def weighted(weights, value):
    return jnp.dot(weights.astype(BF16), with_ones(value), preferred_element_type=F32)


def norm_max(rows):
    rows = rows.reshape(-1, HEAD)
    sums = jnp.dot(rows * rows, jnp.ones((HEAD, HEAD), BF16), preferred_element_type=F32)
    return jnp.max(sums)


def attend_kernel(valid_ref, *refs, frame, pieces, rows, mode):
    refs = list(refs)
    unsafe_in, acc_in = (refs.pop(0), refs.pop(0)) if mode == "more" else (None, None)
    query_in, key_ref, value_ref = refs[:3]
    key_extra, value_extra = refs[3 : 3 + pieces], refs[3 + pieces : 3 + 2 * pieces]
    refs = refs[3 + 2 * pieces :]
    if mode != "own":
        out_ref = refs.pop(0)
    acc, unsafe, keys, values, query_ref, top, key_sem, value_sem, sem = refs
    parts, cuts, blocks, cut_rows = keys.shape[:4]
    tile = blocks * cut_rows

    def fetch(part):
        for cut in range(cuts):
            if part == 0:
                span = pl.ds(frame * rows + cut * cut_rows, cut_rows)
                key, value = key_ref.at[:, span], value_ref.at[:, span]
            else:
                key, value = key_extra[cut].at[part - 1], value_extra[cut].at[part - 1]
            yield (
                pltpu.make_async_copy(key, keys.at[part, cut], key_sem.at[part, cut]),
                pltpu.make_async_copy(value, values.at[part, cut], value_sem.at[part, cut]),
            )

    def start(part):
        for key_copy, value_copy in fetch(part):
            key_copy.start()
            value_copy.start()

    def wait(target, sem, part):
        for cut in range(cuts):
            there = target.at[part, cut]
            pltpu.make_async_copy(there, there, sem.at[part, cut]).wait()

    def rows_of(target, part, cut):
        return target[part, cut].reshape(tile, HEAD)

    def add_part(part, pair, query_norm, assign):
        wait(keys, key_sem, part)
        safe = query_norm * norm_max(keys[part]) * (SCALE * SCALE) <= SAFE * SAFE
        wait(values, value_sem, part)

        @pl.when(safe)
        def _():
            for cut in range(cuts):
                weights = jnp.exp2(score_tile(pair, rows_of(keys, part, cut)))
                sums = weighted(weights, rows_of(values, part, cut))
                acc[...] = sums if assign and cut == 0 else acc[...] + sums

        @pl.when(jnp.logical_not(safe))
        def _():
            unsafe[0] = 1

    query_copy = pltpu.make_async_copy(
        query_in.at[:, pl.ds(frame * rows, rows)], query_ref, sem.at[0]
    )
    query_copy.start()
    if mode == "more":
        acc_copy = pltpu.make_async_copy(acc_in, acc, sem.at[1])
        acc_copy.start()
    else:
        start(0)
    for part in range(1, parts):

        @pl.when(valid_ref[part] > 0)
        def _():
            start(part)

    query_copy.wait()
    query = query_ref[...].reshape(-1, HEAD)
    query_norm = norm_max(query)
    pair = scaled_split(query)
    if mode == "more":
        unsafe[0] = unsafe_in[0]
        acc_copy.wait()
    else:
        unsafe[0] = 0

    if mode == "own":
        add_part(0, pair, query_norm, True)
        return
    if mode == "all":
        acc[...] = jnp.zeros_like(acc)

    def one_part(part, carry):
        @pl.when(valid_ref[part] > 0)
        def _():
            add_part(part, pair, query_norm, False)

        return carry

    lax.fori_loop(1 if mode == "more" else 0, parts, one_part, 0)

    def finish(sums):
        return (sums[:, :HEAD] / sums[:, HEAD:]).astype(BF16)

    @pl.when(unsafe[0] == 0)
    def _():
        out_ref[...] = finish(acc[...]).reshape(out_ref.shape)

    @pl.when(unsafe[0] > 0)
    def _():
        if mode == "more":
            start(0)
            wait(keys, key_sem, 0)
            wait(values, value_sem, 0)

        def one_block(block, carry):
            pair = scaled_split(query_ref[block])
            sums = acc.at[pl.ds(0, rows)]
            sums[...] = jnp.zeros_like(sums)
            top[...] = jnp.full_like(top, LOWEST)

            def slow_part(part, carry):
                @pl.when(valid_ref[part] > 0)
                def _():
                    for cut in range(cuts):
                        scores = score_tile(pair, rows_of(keys, part, cut))
                        old_top = top[:, :1]
                        new_top = jnp.maximum(old_top, jnp.max(scores, axis=1, keepdims=True))
                        part_sums = weighted(
                            jnp.exp2(scores - new_top), rows_of(values, part, cut)
                        )
                        sums[...] = sums[...] * jnp.exp2(old_top - new_top) + part_sums
                        top[...] = jnp.broadcast_to(new_top, top.shape)

                return carry

            lax.fori_loop(0, parts, slow_part, 0)
            out_ref[block] = finish(sums[...])
            return carry

        lax.fori_loop(0, query_ref.shape[0], one_block, 0)


def whole(array):
    return pl.BlockSpec(
        array.shape, lambda i: (0,) * len(array.shape), pipeline_mode=pl.Buffered(1)
    )


def attend(mode, frame, rows, valid, query, key, value, key_extra=(), value_extra=(), own=(), cuts=4):
    blocks = query.shape[0]
    total = blocks * rows
    parts = valid.shape[0]
    pieces = len(key_extra)
    acc = jax.ShapeDtypeStruct((total, 2 * HEAD), F32)
    flag = jax.ShapeDtypeStruct((1,), jnp.int32)
    out = pltpu.HBM((blocks, rows, HEAD), BF16)
    kept = pltpu.VMEM((parts, cuts, blocks, rows // cuts, HEAD), BF16)
    sems = pltpu.SemaphoreType.DMA((parts, cuts))
    scratch = [
        kept, kept, pltpu.VMEM(out.shape, BF16), pltpu.VMEM((rows, HEAD), F32),
        sems, sems, pltpu.SemaphoreType.DMA((2,)),
    ]
    if mode == "own":
        out_shape, out_specs = [acc, flag], [whole(acc), SMEM]
    else:
        out_shape, out_specs = [out], [whole(out)]
        scratch = [pltpu.VMEM(acc.shape, F32), pltpu.SMEM((1,), jnp.int32)] + scratch
    work = {"own": 1, "more": parts - 1, "all": parts}[mode] * total * total
    result = pl.pallas_call(
        functools.partial(attend_kernel, frame=frame, pieces=pieces, rows=rows, mode=mode),
        grid=(1,),
        in_specs=[SMEM, *([SMEM, ANY] if own else []), *[ANY] * (3 + 2 * pieces)],
        out_specs=out_specs,
        out_shape=out_shape,
        scratch_shapes=scratch,
        compiler_params=pltpu.CompilerParams(vmem_limit_bytes=24 << 20),
        cost_estimate=pl.CostEstimate(
            flops=4 * work * HEAD, bytes_accessed=16 * total * HEAD, transcendentals=work
        ),
    )(valid, *own[::-1], query, key, value, *key_extra, *value_extra)
    return result if mode == "own" else result[0]


def piece_rows(keyframe, piece, shape):
    frames, rows, cuts = shape
    start = lax.rem(keyframe, frames) * rows + piece * (rows // cuts)
    return pl.ds(pl.multiple_of(start, rows // cuts), rows // cuts)


def run_copies(copies):
    for copy in copies:
        copy.start()
    for copy in copies:
        copy.wait()


def cut_kernel(place_ref, keyframes_ref, source_ref, *refs, shape):
    *out_refs, sem = refs
    x = place_ref[0] // 2
    copies = []
    for step, out_ref in enumerate(out_refs, 1):
        for j in range(out_ref.shape[0]):
            rows = piece_rows(keyframes_ref[j], lax.rem(x + step, shape[2]), shape)
            copies.append(
                pltpu.make_async_copy(source_ref.at[:, rows], out_ref.at[j], sem.at[len(copies)])
            )
    run_copies(copies)


def pick_x_kernel(place_ref, keyframes_ref, source_ref, *refs, shape):
    *got_refs, out_ref, sem = refs
    x = place_ref[0] // 2
    extras = out_ref.shape[0]
    for j in range(extras):
        keyframe = keyframes_ref[j]
        step = lax.rem(x - keyframe // (2 * shape[0]) + shape[2], shape[2])

        @pl.when(step == 0)
        def _():
            rows = piece_rows(keyframe, x, shape)
            pltpu.make_async_copy(source_ref.at[:, rows], out_ref.at[j], sem.at[j]).start()

        for which, got_ref in enumerate(got_refs, 1):

            @pl.when(step == which)
            def _():
                pltpu.make_async_copy(got_ref.at[j], out_ref.at[j], sem.at[j]).start()

    for j in range(extras):
        pltpu.make_async_copy(got_refs[0].at[j], out_ref.at[j], sem.at[j]).wait()


def pick_y_kernel(place_ref, keyframes_ref, mine_ref, other_ref, out_ref, sem, *, shape):
    y = lax.rem(place_ref[0], 2)
    extras = out_ref.shape[0]
    for j in range(extras):
        mine, other = mine_ref.at[j], other_ref.at[j]
        same = lax.rem(keyframes_ref[j] // shape[0], 2) == y

        @pl.when(same)
        def _():
            pltpu.make_async_copy(mine, out_ref.at[j], sem.at[j]).start()

        @pl.when(jnp.logical_not(same))
        def _():
            pltpu.make_async_copy(other, out_ref.at[j], sem.at[j]).start()

    for j in range(extras):
        pltpu.make_async_copy(out_ref.at[j], out_ref.at[j], sem.at[j]).wait()


def move_call(kernel, out_shapes, place, keyframes, *arrays):
    moved = sum(math.prod(o.shape) for o in out_shapes)
    return pl.pallas_call(
        kernel,
        grid=(1,),
        in_specs=[SMEM, SMEM] + [ANY] * len(arrays),
        out_specs=[whole(o) for o in out_shapes],
        out_shape=out_shapes,
        scratch_shapes=[pltpu.SemaphoreType.DMA((len(out_shapes) * keyframes.shape[0] + 1,))],
        compiler_params=pltpu.CompilerParams(vmem_limit_bytes=8 << 20),
        cost_estimate=pl.CostEstimate(flops=0, bytes_accessed=4 * moved, transcendentals=0),
    )(place, keyframes, *arrays)


def swap_branch(value):
    return lax.ppermute(value, "branch", [(0, 1), (1, 0)])


def to_heads(value):
    return lax.all_to_all(value, "seq", split_axis=0, concat_axis=0, tiled=True)


def shift_x(value, step):
    size = lax.axis_size("mp")
    return lax.ppermute(value, "mp", [(m, (m + 2 * step) % size) for m in range(size)])


def flip_y(value):
    size = lax.axis_size("mp")
    return lax.ppermute(value, "mp", [(m, m ^ 1) for m in range(size)])


def spread_along_x(place, keyframes, source, shape):
    piece = (keyframes.shape[0], source.shape[0], shape[1] // shape[2], HEAD)
    piece = jax.ShapeDtypeStruct(piece, BF16)
    cuts = move_call(
        functools.partial(cut_kernel, shape=shape),
        [piece] * (shape[2] - 1), place, keyframes, source,
    )
    got = [shift_x(cut, step) for step, cut in enumerate(cuts, 1)]
    return move_call(
        functools.partial(pick_x_kernel, shape=shape),
        [piece], place, keyframes, source, *got,
    )[0]


def spread_from_x(place, keyframes, mine, shape):
    other = flip_y(mine)
    (mine,) = move_call(
        functools.partial(pick_y_kernel, shape=shape),
        [jax.ShapeDtypeStruct(mine.shape, BF16)], place, keyframes, mine, other,
    )
    return [mine] + [shift_x(mine, step) for step in range(1, shape[2])]


def local(queries, keys, values, inject, keyframes, key_mask):
    queries, keys, values = queries[0], keys[0], values[0]
    frames, rows, _ = queries.shape
    shape = (frames, rows, lax.axis_size("mp") // 2)
    place = lax.axis_index("mp").astype(jnp.int32).reshape(1)
    partner_keys = swap_branch(keys)
    partner_queries = swap_branch(queries)

    value_rows = split_heads(values).reshape(-1, frames * rows, HEAD)
    value_heads = to_heads(value_rows)
    value_mine = spread_along_x(place, keyframes, value_heads, shape)
    value_extra = spread_from_x(place, keyframes, value_mine, shape)

    key_rows = blend_heads(inject, keys, partner_keys)
    key_heads = to_heads(key_rows)
    key_mine = spread_along_x(place, keyframes, key_heads, shape)
    key_extra = spread_from_x(place, keyframes, key_mine, shape)

    query_rows = blend_heads(inject, queries, partner_queries)
    query_heads = to_heads(query_rows)
    outs = []
    always = jnp.ones((1,), jnp.int32)
    for f in range(frames):
        masks = lax.dynamic_index_in_dim(key_mask, place[0] * frames + f, 0, keepdims=False)
        valid = jnp.concatenate([always, masks])
        heads = (query_heads, key_heads, value_heads)
        extra = (key_extra, value_extra)
        if f == 0:
            own = attend("own", f, rows, always, *heads)
            out = attend("more", f, rows, valid, *heads, *extra, own)
        else:
            out = attend("all", f, rows, valid, *heads, *extra)
        back = to_heads(out)
        outs.append(back.transpose(1, 0, 2).reshape(rows, -1))
    return jnp.stack(outs)[None]


def solution(mesh):
    return jax.shard_map(
        local,
        mesh=mesh,
        in_specs=(
            P("branch", "mp", "seq", None),
            P("branch", "mp", "seq", None),
            P("branch", "mp", "seq", None),
            P("branch", None),
            P(),
            P(),
        ),
        out_specs=P("branch", "mp", "seq", None),
        check_vma=False,
    )
```

```python
import functools
import math

import jax
import jax.numpy as jnp
from jax import lax
from jax.experimental import pallas as pl
from jax.experimental.pallas import tpu as pltpu
from jax.sharding import PartitionSpec as P


HEAD = 128
SCALE = math.log2(math.e) / math.sqrt(HEAD)
SAFE = 100.0
LOWEST = -1e30
BF16 = jnp.bfloat16
F32 = jnp.float32


ANY = pl.BlockSpec(memory_space=pl.ANY)
SMEM = pl.BlockSpec(memory_space=pltpu.SMEM)


def blend_kernel(strength_ref, own_ref, partner_ref, out_ref, *, heads):
    first = pl.program_id(0) * heads
    for head in range(heads):
        share = strength_ref[0, first + head]
        lanes = slice(head * HEAD, (head + 1) * HEAD)
        mixed = (1.0 - share) * own_ref[:, :, lanes].astype(F32) + share * partner_ref[
            :, :, lanes
        ].astype(F32)
        out_ref[head] = mixed.astype(BF16).reshape(-1, HEAD)


def blend_heads(strength, own, partner, steps=2):
    frames, rows, width = own.shape
    heads = width // HEAD
    group = heads // steps
    block = pl.BlockSpec((frames, rows, group * HEAD), lambda h: (0, 0, h))
    return pl.pallas_call(
        functools.partial(blend_kernel, heads=group),
        grid=(steps,),
        in_specs=[SMEM, block, block],
        out_specs=pl.BlockSpec((group, frames * rows, HEAD), lambda h: (h, 0, 0)),
        out_shape=jax.ShapeDtypeStruct((heads, frames * rows, HEAD), BF16),
        cost_estimate=pl.CostEstimate(
            flops=3 * own.size, bytes_accessed=6 * own.size, transcendentals=0
        ),
        name="blend",
    )(strength, own, partner)


def split_kernel(source_ref, out_ref, kept_ref, in_sem, out_sem):
    heads = out_ref.shape[0]
    reads, writes = [], []
    for head in range(heads):
        lanes = pl.ds(head * HEAD, HEAD)
        kept = kept_ref.at[head]
        reads.append(pltpu.make_async_copy(source_ref.at[:, :, lanes], kept, in_sem.at[head]))
        writes.append(pltpu.make_async_copy(kept, out_ref.at[head], out_sem.at[head]))
    for read in reads:
        read.start()
    for read, write in zip(reads, writes):
        read.wait()
        write.start()
    for write in writes:
        write.wait()


def split_heads(rows):
    frames, count, width = rows.shape
    heads = width // HEAD
    shape = (heads, frames, count, HEAD)
    sems = pltpu.SemaphoreType.DMA((heads,))
    return pl.pallas_call(
        split_kernel,
        in_specs=[ANY],
        out_specs=ANY,
        out_shape=pltpu.HBM(shape, BF16),
        scratch_shapes=[pltpu.VMEM(shape, BF16), sems, sems],
        cost_estimate=pl.CostEstimate(flops=0, bytes_accessed=4 * rows.size, transcendentals=0),
        name="split_heads",
    )(rows)


def dot_nt(a, b):
    return lax.dot_general(a, b, (((1,), (1,)), ((), ())), preferred_element_type=F32)


def scaled_split(query):
    scaled = query.astype(F32) * SCALE
    high = scaled.astype(BF16)
    low = (scaled - high.astype(F32)).astype(BF16)
    return jnp.concatenate([high, low], axis=1)


def score_tile(query_pair, key):
    return dot_nt(query_pair, jnp.concatenate([key, key], axis=1))


def with_ones(value):
    return jnp.concatenate([value, jnp.ones_like(value)], axis=1)


def weighted(weights, value):
    return jnp.dot(weights.astype(BF16), with_ones(value), preferred_element_type=F32)


def norm_max(rows):
    rows = rows.reshape(-1, HEAD)
    sums = jnp.dot(rows * rows, jnp.ones((HEAD, HEAD), BF16), preferred_element_type=F32)
    return jnp.max(sums)


def attend_kernel(valid_ref, *refs, frame, pieces, rows, mode):
    refs = list(refs)
    unsafe_in, acc_in = (refs.pop(0), refs.pop(0)) if mode == "more" else (None, None)
    query_in, key_ref, value_ref = refs[:3]
    key_extra, value_extra = refs[3 : 3 + pieces], refs[3 + pieces : 3 + 2 * pieces]
    refs = refs[3 + 2 * pieces :]
    if mode != "own":
        out_ref = refs.pop(0)
    if mode == "more":
        own_sums = refs.pop()
    acc, unsafe, keys, values, query_ref, top, key_sem, value_sem, sem = refs
    parts, cuts, blocks, cut_rows = keys.shape[:4]
    tile = blocks * cut_rows

    def fetch(part):
        for cut in range(cuts):
            if part == 0:
                span = pl.ds(frame * rows + cut * cut_rows, cut_rows)
                key, value = key_ref.at[:, span], value_ref.at[:, span]
            else:
                key, value = key_extra[cut].at[part - 1], value_extra[cut].at[part - 1]
            yield (
                pltpu.make_async_copy(key, keys.at[part, cut], key_sem.at[part, cut]),
                pltpu.make_async_copy(value, values.at[part, cut], value_sem.at[part, cut]),
            )

    def start(part):
        for key_copy, value_copy in fetch(part):
            key_copy.start()
            value_copy.start()

    def wait(target, sem, part):
        for cut in range(cuts):
            there = target.at[part, cut]
            pltpu.make_async_copy(there, there, sem.at[part, cut]).wait()

    def rows_of(target, part, cut):
        return target[part, cut].reshape(tile, HEAD)

    def add_part(part, pair, query_norm, assign):
        wait(keys, key_sem, part)
        safe = query_norm * norm_max(keys[part]) * (SCALE * SCALE) <= SAFE * SAFE
        wait(values, value_sem, part)

        @pl.when(safe)
        def _():
            for cut in range(cuts):
                weights = jnp.exp2(score_tile(pair, rows_of(keys, part, cut)))
                sums = weighted(weights, rows_of(values, part, cut))
                acc[...] = sums if assign and cut == 0 else acc[...] + sums

        @pl.when(jnp.logical_not(safe))
        def _():
            unsafe[0] = 1

    query_copy = pltpu.make_async_copy(
        query_in.at[:, pl.ds(frame * rows, rows)], query_ref, sem.at[0]
    )
    query_copy.start()
    if mode == "more":
        acc_copy = pltpu.make_async_copy(acc_in, own_sums, sem.at[1])
        acc_copy.start()
    else:
        start(0)
    for part in range(1, parts):

        @pl.when(valid_ref[part] > 0)
        def _():
            start(part)

    query_copy.wait()
    query = query_ref[...].reshape(-1, HEAD)
    query_norm = norm_max(query)
    pair = scaled_split(query)
    if mode == "more":
        unsafe[0] = unsafe_in[0]
    else:
        unsafe[0] = 0

    if mode == "own":
        add_part(0, pair, query_norm, True)
        return
    acc[...] = jnp.zeros_like(acc)

    def one_part(part, carry):
        @pl.when(valid_ref[part] > 0)
        def _():
            add_part(part, pair, query_norm, False)

        return carry

    lax.fori_loop(1 if mode == "more" else 0, parts, one_part, 0)

    def finish(sums):
        return (sums[:, :HEAD] / sums[:, HEAD:]).astype(BF16)

    if mode == "more":
        acc_copy.wait()

    @pl.when(unsafe[0] == 0)
    def _():
        sums = acc[...] + own_sums[...] if mode == "more" else acc[...]
        out_ref[...] = finish(sums).reshape(out_ref.shape)

    @pl.when(unsafe[0] > 0)
    def _():
        if mode == "more":
            start(0)
            wait(keys, key_sem, 0)
            wait(values, value_sem, 0)

        def one_block(block, carry):
            pair = scaled_split(query_ref[block])
            sums = acc.at[pl.ds(0, rows)]
            sums[...] = jnp.zeros_like(sums)
            top[...] = jnp.full_like(top, LOWEST)

            def slow_part(part, carry):
                @pl.when(valid_ref[part] > 0)
                def _():
                    for cut in range(cuts):
                        scores = score_tile(pair, rows_of(keys, part, cut))
                        old_top = top[:, :1]
                        new_top = jnp.maximum(old_top, jnp.max(scores, axis=1, keepdims=True))
                        part_sums = weighted(
                            jnp.exp2(scores - new_top), rows_of(values, part, cut)
                        )
                        sums[...] = sums[...] * jnp.exp2(old_top - new_top) + part_sums
                        top[...] = jnp.broadcast_to(new_top, top.shape)

                return carry

            lax.fori_loop(0, parts, slow_part, 0)
            out_ref[block] = finish(sums[...])
            return carry

        lax.fori_loop(0, query_ref.shape[0], one_block, 0)


def whole(array):
    return pl.BlockSpec(
        array.shape, lambda i: (0,) * len(array.shape), pipeline_mode=pl.Buffered(1)
    )


def attend(mode, frame, rows, valid, query, key, value, key_extra=(), value_extra=(), own=(), cuts=4):
    blocks = query.shape[0]
    total = blocks * rows
    parts = valid.shape[0]
    pieces = len(key_extra)
    acc = jax.ShapeDtypeStruct((total, 2 * HEAD), F32)
    flag = jax.ShapeDtypeStruct((1,), jnp.int32)
    out = pltpu.HBM((blocks, rows, HEAD), BF16)
    kept = pltpu.VMEM((parts, cuts, blocks, rows // cuts, HEAD), BF16)
    sems = pltpu.SemaphoreType.DMA((parts, cuts))
    scratch = [
        kept, kept, pltpu.VMEM(out.shape, BF16), pltpu.VMEM((rows, HEAD), F32),
        sems, sems, pltpu.SemaphoreType.DMA((2,)),
    ]
    if mode == "own":
        out_shape, out_specs = [acc, flag], [whole(acc), SMEM]
    else:
        out_shape, out_specs = [out], [whole(out)]
        scratch = [pltpu.VMEM(acc.shape, F32), pltpu.SMEM((1,), jnp.int32)] + scratch
    if mode == "more":
        scratch.append(pltpu.VMEM(acc.shape, F32))
    work = {"own": 1, "more": parts - 1, "all": parts}[mode] * total * total
    result = pl.pallas_call(
        functools.partial(attend_kernel, frame=frame, pieces=pieces, rows=rows, mode=mode),
        grid=(1,),
        in_specs=[SMEM, *([SMEM, ANY] if own else []), *[ANY] * (3 + 2 * pieces)],
        out_specs=out_specs,
        out_shape=out_shape,
        scratch_shapes=scratch,
        compiler_params=pltpu.CompilerParams(vmem_limit_bytes=24 << 20),
        cost_estimate=pl.CostEstimate(
            flops=4 * work * HEAD, bytes_accessed=16 * total * HEAD, transcendentals=work
        ),
    )(valid, *own[::-1], query, key, value, *key_extra, *value_extra)
    return result if mode == "own" else result[0]


def piece_rows(keyframe, piece, shape):
    frames, rows, cuts = shape
    start = lax.rem(keyframe, frames) * rows + piece * (rows // cuts)
    return pl.ds(pl.multiple_of(start, rows // cuts), rows // cuts)


def run_copies(copies):
    for copy in copies:
        copy.start()
    for copy in copies:
        copy.wait()


def cut_kernel(place_ref, keyframes_ref, source_ref, *refs, shape):
    *out_refs, sem = refs
    x = place_ref[0] // 2
    copies = []
    for step, out_ref in enumerate(out_refs, 1):
        for j in range(out_ref.shape[0]):
            rows = piece_rows(keyframes_ref[j], lax.rem(x + step, shape[2]), shape)
            copies.append(
                pltpu.make_async_copy(source_ref.at[:, rows], out_ref.at[j], sem.at[len(copies)])
            )
    run_copies(copies)


def pick_x_kernel(place_ref, keyframes_ref, source_ref, *refs, shape):
    *got_refs, out_ref, sem = refs
    x = place_ref[0] // 2
    extras = out_ref.shape[0]
    for j in range(extras):
        keyframe = keyframes_ref[j]
        step = lax.rem(x - keyframe // (2 * shape[0]) + shape[2], shape[2])

        @pl.when(step == 0)
        def _():
            rows = piece_rows(keyframe, x, shape)
            pltpu.make_async_copy(source_ref.at[:, rows], out_ref.at[j], sem.at[j]).start()

        for which, got_ref in enumerate(got_refs, 1):

            @pl.when(step == which)
            def _():
                pltpu.make_async_copy(got_ref.at[j], out_ref.at[j], sem.at[j]).start()

    for j in range(extras):
        pltpu.make_async_copy(got_refs[0].at[j], out_ref.at[j], sem.at[j]).wait()


def pick_y_kernel(place_ref, keyframes_ref, mine_ref, other_ref, out_ref, sem, *, shape):
    y = lax.rem(place_ref[0], 2)
    extras = out_ref.shape[0]
    for j in range(extras):
        mine, other = mine_ref.at[j], other_ref.at[j]
        same = lax.rem(keyframes_ref[j] // shape[0], 2) == y

        @pl.when(same)
        def _():
            pltpu.make_async_copy(mine, out_ref.at[j], sem.at[j]).start()

        @pl.when(jnp.logical_not(same))
        def _():
            pltpu.make_async_copy(other, out_ref.at[j], sem.at[j]).start()

    for j in range(extras):
        pltpu.make_async_copy(out_ref.at[j], out_ref.at[j], sem.at[j]).wait()


def move_call(kernel, out_shapes, place, keyframes, *arrays):
    moved = sum(math.prod(o.shape) for o in out_shapes)
    return pl.pallas_call(
        kernel,
        in_specs=[SMEM, SMEM] + [ANY] * len(arrays),
        out_specs=[pl.BlockSpec(memory_space=pltpu.VMEM)] * len(out_shapes),
        out_shape=[pltpu.VMEM(o.shape, o.dtype) for o in out_shapes],
        scratch_shapes=[pltpu.SemaphoreType.DMA((len(out_shapes) * keyframes.shape[0] + 1,))],
        compiler_params=pltpu.CompilerParams(vmem_limit_bytes=8 << 20),
        cost_estimate=pl.CostEstimate(flops=0, bytes_accessed=4 * moved, transcendentals=0),
    )(place, keyframes, *arrays)


def swap_branch(value):
    return lax.ppermute(value, "branch", [(0, 1), (1, 0)])


def to_heads(value):
    return lax.all_to_all(value, "seq", split_axis=0, concat_axis=0, tiled=True)


def shift_x(value, step):
    size = lax.axis_size("mp")
    return lax.ppermute(value, "mp", [(m, (m + 2 * step) % size) for m in range(size)])


def flip_y(value):
    size = lax.axis_size("mp")
    return lax.ppermute(value, "mp", [(m, m ^ 1) for m in range(size)])


def spread_along_x(place, keyframes, source, shape):
    piece = (keyframes.shape[0], source.shape[0], shape[1] // shape[2], HEAD)
    piece = jax.ShapeDtypeStruct(piece, BF16)
    cuts = move_call(
        functools.partial(cut_kernel, shape=shape),
        [piece] * (shape[2] - 1), place, keyframes, source,
    )
    got = [shift_x(cut, step) for step, cut in enumerate(cuts, 1)]
    return move_call(
        functools.partial(pick_x_kernel, shape=shape),
        [piece], place, keyframes, source, *got,
    )[0]


def spread_from_x(place, keyframes, mine, shape):
    other = flip_y(mine)
    (mine,) = move_call(
        functools.partial(pick_y_kernel, shape=shape),
        [jax.ShapeDtypeStruct(mine.shape, BF16)], place, keyframes, mine, other,
    )
    return [mine] + [shift_x(mine, step) for step in range(1, shape[2])]


def local(queries, keys, values, inject, keyframes, key_mask):
    queries, keys, values = queries[0], keys[0], values[0]
    frames, rows, _ = queries.shape
    shape = (frames, rows, lax.axis_size("mp") // 2)
    place = lax.axis_index("mp").astype(jnp.int32).reshape(1)
    partner_keys = swap_branch(keys)
    partner_queries = swap_branch(queries)

    value_rows = split_heads(values).reshape(-1, frames * rows, HEAD)
    value_heads = to_heads(value_rows)
    value_mine = spread_along_x(place, keyframes, value_heads, shape)
    value_extra = spread_from_x(place, keyframes, value_mine, shape)

    key_rows = blend_heads(inject, keys, partner_keys)
    key_heads = to_heads(key_rows)
    key_mine = spread_along_x(place, keyframes, key_heads, shape)
    key_extra = spread_from_x(place, keyframes, key_mine, shape)

    query_rows = blend_heads(inject, queries, partner_queries)
    query_heads = to_heads(query_rows)
    outs = []
    always = jnp.ones((1,), jnp.int32)
    for f in range(frames):
        masks = lax.dynamic_index_in_dim(key_mask, place[0] * frames + f, 0, keepdims=False)
        valid = jnp.concatenate([always, masks])
        heads = (query_heads, key_heads, value_heads)
        extra = (key_extra, value_extra)
        if f == 0:
            own = attend("own", f, rows, always, *heads)
            out = attend("more", f, rows, valid, *heads, *extra, own)
        else:
            out = attend("all", f, rows, valid, *heads, *extra)
        back = to_heads(out)
        outs.append(back.transpose(1, 0, 2).reshape(rows, -1))
    return jnp.stack(outs)[None]


def solution(mesh):
    return jax.shard_map(
        local,
        mesh=mesh,
        in_specs=(
            P("branch", "mp", "seq", None),
            P("branch", "mp", "seq", None),
            P("branch", "mp", "seq", None),
            P("branch", None),
            P(),
            P(),
        ),
        out_specs=P("branch", "mp", "seq", None),
        check_vma=False,
    )
```

```python
import functools
import math

import jax
import jax.numpy as jnp
from jax import lax
from jax.experimental import pallas as pl
from jax.experimental.pallas import tpu as pltpu
from jax.sharding import PartitionSpec as P


HEAD = 128
SCALE = math.log2(math.e) / math.sqrt(HEAD)
SAFE = 100.0
LOWEST = -1e30
BF16 = jnp.bfloat16
F32 = jnp.float32


ANY = pl.BlockSpec(memory_space=pl.ANY)
SMEM = pl.BlockSpec(memory_space=pltpu.SMEM)
VMEM = pl.BlockSpec(memory_space=pltpu.VMEM)


def blend_kernel(strength_ref, own_ref, partner_ref, out_ref, *, heads):
    first = pl.program_id(0) * heads
    for head in range(heads):
        share = strength_ref[0, first + head]
        lanes = slice(head * HEAD, (head + 1) * HEAD)
        mixed = (1.0 - share) * own_ref[:, :, lanes].astype(F32) + share * partner_ref[
            :, :, lanes
        ].astype(F32)
        out_ref[head] = mixed.astype(BF16).reshape(-1, HEAD)


def blend_heads(strength, own, partner, steps=2):
    frames, rows, width = own.shape
    heads = width // HEAD
    group = heads // steps
    block = pl.BlockSpec((frames, rows, group * HEAD), lambda h: (0, 0, h))
    return pl.pallas_call(
        functools.partial(blend_kernel, heads=group),
        grid=(steps,),
        in_specs=[SMEM, block, block],
        out_specs=pl.BlockSpec((group, frames * rows, HEAD), lambda h: (h, 0, 0)),
        out_shape=jax.ShapeDtypeStruct((heads, frames * rows, HEAD), BF16),
        cost_estimate=pl.CostEstimate(
            flops=3 * own.size, bytes_accessed=6 * own.size, transcendentals=0
        ),
        name="blend",
    )(strength, own, partner)


def split_kernel(source_ref, out_ref, kept_ref, in_sem, out_sem):
    heads = out_ref.shape[0]
    reads, writes = [], []
    for head in range(heads):
        lanes = pl.ds(head * HEAD, HEAD)
        kept = kept_ref.at[head]
        reads.append(pltpu.make_async_copy(source_ref.at[:, :, lanes], kept, in_sem.at[head]))
        writes.append(pltpu.make_async_copy(kept, out_ref.at[head], out_sem.at[head]))
    for read in reads:
        read.start()
    for read, write in zip(reads, writes):
        read.wait()
        write.start()
    for write in writes:
        write.wait()


def split_heads(rows):
    frames, count, width = rows.shape
    heads = width // HEAD
    shape = (heads, frames, count, HEAD)
    sems = pltpu.SemaphoreType.DMA((heads,))
    return pl.pallas_call(
        split_kernel,
        in_specs=[ANY],
        out_specs=ANY,
        out_shape=pltpu.HBM(shape, BF16),
        scratch_shapes=[pltpu.VMEM(shape, BF16), sems, sems],
        cost_estimate=pl.CostEstimate(flops=0, bytes_accessed=4 * rows.size, transcendentals=0),
        name="split_heads",
    )(rows)


def dot_nt(a, b):
    return lax.dot_general(a, b, (((1,), (1,)), ((), ())), preferred_element_type=F32)


def scaled_split(query):
    scaled = query.astype(F32) * SCALE
    high = scaled.astype(BF16)
    low = (scaled - high.astype(F32)).astype(BF16)
    return jnp.concatenate([high, low], axis=1)


def score_tile(query_pair, key):
    return dot_nt(query_pair, jnp.concatenate([key, key], axis=1))


def with_ones(value):
    return jnp.concatenate([value, jnp.ones_like(value)], axis=1)


def weighted(weights, value):
    return jnp.dot(weights.astype(BF16), with_ones(value), preferred_element_type=F32)


def norm_max(rows):
    rows = rows.reshape(-1, HEAD)
    sums = jnp.dot(rows * rows, jnp.ones((HEAD, HEAD), BF16), preferred_element_type=F32)
    return jnp.max(sums)


def attend_kernel(valid_ref, *refs, frame, pieces, rows, mode):
    refs = list(refs)
    unsafe_in, acc_in = (refs.pop(0), refs.pop(0)) if mode == "more" else (None, None)
    query_in, key_ref, value_ref = refs[:3]
    key_extra, value_extra = refs[3 : 3 + pieces], refs[3 + pieces : 3 + 2 * pieces]
    refs = refs[3 + 2 * pieces :]
    if mode != "own":
        out_ref = refs.pop(0)
    if mode == "more":
        own_sums = refs.pop()
    acc, unsafe, keys, values, query_ref, top, key_sem, value_sem, sem = refs
    parts, cuts, blocks, cut_rows = keys.shape[:4]
    tile = blocks * cut_rows

    def fetch(part):
        for cut in range(cuts):
            if part == 0:
                span = pl.ds(frame * rows + cut * cut_rows, cut_rows)
                key, value = key_ref.at[:, span], value_ref.at[:, span]
            else:
                key, value = key_extra[cut].at[part - 1], value_extra[cut].at[part - 1]
            yield (
                pltpu.make_async_copy(key, keys.at[part, cut], key_sem.at[part, cut]),
                pltpu.make_async_copy(value, values.at[part, cut], value_sem.at[part, cut]),
            )

    def start(part):
        for key_copy, value_copy in fetch(part):
            key_copy.start()
            value_copy.start()

    def wait(target, sem, part):
        for cut in range(cuts):
            there = target.at[part, cut]
            pltpu.make_async_copy(there, there, sem.at[part, cut]).wait()

    def rows_of(target, part, cut):
        return target[part, cut].reshape(tile, HEAD)

    def add_part(part, pair, query_norm, assign):
        wait(keys, key_sem, part)
        safe = query_norm * norm_max(keys[part]) * (SCALE * SCALE) <= SAFE * SAFE
        wait(values, value_sem, part)

        @pl.when(safe)
        def _():
            for cut in range(cuts):
                weights = jnp.exp2(score_tile(pair, rows_of(keys, part, cut)))
                sums = weighted(weights, rows_of(values, part, cut))
                acc[...] = sums if assign and cut == 0 else acc[...] + sums

        @pl.when(jnp.logical_not(safe))
        def _():
            unsafe[0] = 1

    query_copy = pltpu.make_async_copy(
        query_in.at[:, pl.ds(frame * rows, rows)], query_ref, sem.at[0]
    )
    query_copy.start()
    if mode == "more":
        acc_copy = pltpu.make_async_copy(acc_in, own_sums, sem.at[1])
        acc_copy.start()
    else:
        start(0)
    for part in range(1, parts):

        @pl.when(valid_ref[part] > 0)
        def _():
            start(part)

    query_copy.wait()
    query = query_ref[...].reshape(-1, HEAD)
    query_norm = norm_max(query)
    pair = scaled_split(query)
    if mode == "more":
        unsafe[0] = unsafe_in[0]
    else:
        unsafe[0] = 0

    if mode == "own":
        add_part(0, pair, query_norm, True)
        return
    acc[...] = jnp.zeros_like(acc)

    def one_part(part, carry):
        @pl.when(valid_ref[part] > 0)
        def _():
            add_part(part, pair, query_norm, False)

        return carry

    lax.fori_loop(1 if mode == "more" else 0, parts, one_part, 0)

    def finish(sums):
        return (sums[:, :HEAD] / sums[:, HEAD:]).astype(BF16)

    if mode == "more":
        acc_copy.wait()

    @pl.when(unsafe[0] == 0)
    def _():
        sums = acc[...] + own_sums[...] if mode == "more" else acc[...]
        out_ref[...] = finish(sums).reshape(out_ref.shape)

    @pl.when(unsafe[0] > 0)
    def _():
        if mode == "more":
            start(0)
            wait(keys, key_sem, 0)
            wait(values, value_sem, 0)

        def one_block(block, carry):
            pair = scaled_split(query_ref[block])
            sums = acc.at[pl.ds(0, rows)]
            sums[...] = jnp.zeros_like(sums)
            top[...] = jnp.full_like(top, LOWEST)

            def slow_part(part, carry):
                @pl.when(valid_ref[part] > 0)
                def _():
                    for cut in range(cuts):
                        scores = score_tile(pair, rows_of(keys, part, cut))
                        old_top = top[:, :1]
                        new_top = jnp.maximum(old_top, jnp.max(scores, axis=1, keepdims=True))
                        part_sums = weighted(
                            jnp.exp2(scores - new_top), rows_of(values, part, cut)
                        )
                        sums[...] = sums[...] * jnp.exp2(old_top - new_top) + part_sums
                        top[...] = jnp.broadcast_to(new_top, top.shape)

                return carry

            lax.fori_loop(0, parts, slow_part, 0)
            out_ref[block] = finish(sums[...])
            return carry

        lax.fori_loop(0, query_ref.shape[0], one_block, 0)


def whole(array):
    return pl.BlockSpec(
        array.shape, lambda i: (0,) * len(array.shape), pipeline_mode=pl.Buffered(1)
    )


def attend(mode, frame, rows, valid, query, key, value, key_extra=(), value_extra=(), own=(), cuts=4):
    blocks = query.shape[0]
    total = blocks * rows
    parts = valid.shape[0]
    pieces = len(key_extra)
    acc = jax.ShapeDtypeStruct((total, 2 * HEAD), F32)
    flag = jax.ShapeDtypeStruct((1,), jnp.int32)
    out = pltpu.HBM((blocks, rows, HEAD), BF16)
    kept = pltpu.VMEM((parts, cuts, blocks, rows // cuts, HEAD), BF16)
    sems = pltpu.SemaphoreType.DMA((parts, cuts))
    scratch = [
        kept, kept, pltpu.VMEM(out.shape, BF16), pltpu.VMEM((rows, HEAD), F32),
        sems, sems, pltpu.SemaphoreType.DMA((2,)),
    ]
    if mode == "own":
        out_shape, out_specs = [acc, flag], [whole(acc), SMEM]
    else:
        out_shape, out_specs = [out], [whole(out)]
        scratch = [pltpu.VMEM(acc.shape, F32), pltpu.SMEM((1,), jnp.int32)] + scratch
    if mode == "more":
        scratch.append(pltpu.VMEM(acc.shape, F32))
    work = {"own": 1, "more": parts - 1, "all": parts}[mode] * total * total
    result = pl.pallas_call(
        functools.partial(attend_kernel, frame=frame, pieces=pieces, rows=rows, mode=mode),
        grid=(1,),
        in_specs=[SMEM, *([SMEM, ANY] if own else []), *[ANY] * (3 + 2 * pieces)],
        out_specs=out_specs,
        out_shape=out_shape,
        scratch_shapes=scratch,
        compiler_params=pltpu.CompilerParams(vmem_limit_bytes=24 << 20),
        cost_estimate=pl.CostEstimate(
            flops=4 * work * HEAD, bytes_accessed=16 * total * HEAD, transcendentals=work
        ),
    )(valid, *own[::-1], query, key, value, *key_extra, *value_extra)
    return result if mode == "own" else result[0]


def piece_rows(keyframe, piece, shape):
    frames, rows, cuts = shape
    start = lax.rem(keyframe, frames) * rows + piece * (rows // cuts)
    return pl.ds(pl.multiple_of(start, rows // cuts), rows // cuts)


def run_copies(copies):
    for copy in copies:
        copy.start()
    for copy in copies:
        copy.wait()


def cut_kernel(place_ref, keyframes_ref, source_ref, *refs, shape):
    *out_refs, sem = refs
    x = place_ref[0] // 2
    copies = []
    for step, out_ref in enumerate(out_refs, 1):
        for j in range(out_ref.shape[0]):
            rows = piece_rows(keyframes_ref[j], lax.rem(x + step, shape[2]), shape)
            copies.append(
                pltpu.make_async_copy(source_ref.at[:, rows], out_ref.at[j], sem.at[len(copies)])
            )
    run_copies(copies)


def pick_x_kernel(place_ref, keyframes_ref, source_ref, *refs, shape):
    *got_refs, out_ref, sem = refs
    x = place_ref[0] // 2
    for j in range(out_ref.shape[0]):
        keyframe = keyframes_ref[j]
        step = lax.rem(x - keyframe // (2 * shape[0]) + shape[2], shape[2])

        @pl.when(step == 0)
        def _():
            rows = piece_rows(keyframe, x, shape)
            run_copies([pltpu.make_async_copy(source_ref.at[:, rows], out_ref.at[j], sem.at[j])])

        for which, got_ref in enumerate(got_refs, 1):

            @pl.when(step == which)
            def _():
                out_ref[j] = got_ref[j]


def pick_y_kernel(place_ref, keyframes_ref, mine_ref, other_ref, out_ref, sem, *, shape):
    y = lax.rem(place_ref[0], 2)
    for j in range(out_ref.shape[0]):
        same = lax.rem(keyframes_ref[j] // shape[0], 2) == y

        @pl.when(same)
        def _():
            out_ref[j] = mine_ref[j]

        @pl.when(jnp.logical_not(same))
        def _():
            out_ref[j] = other_ref[j]


def move_call(kernel, out_shapes, place, keyframes, *arrays):
    moved = sum(math.prod(o.shape) for o in out_shapes)
    return pl.pallas_call(
        kernel,
        in_specs=[SMEM, SMEM] + [VMEM if a.ndim == 4 else ANY for a in arrays],
        out_specs=[VMEM] * len(out_shapes),
        out_shape=[pltpu.VMEM(o.shape, o.dtype) for o in out_shapes],
        scratch_shapes=[pltpu.SemaphoreType.DMA((len(out_shapes) * keyframes.shape[0] + 1,))],
        compiler_params=pltpu.CompilerParams(vmem_limit_bytes=8 << 20),
        cost_estimate=pl.CostEstimate(flops=0, bytes_accessed=4 * moved, transcendentals=0),
    )(place, keyframes, *arrays)


def swap_branch(value):
    return lax.ppermute(value, "branch", [(0, 1), (1, 0)])


def to_heads(value):
    return lax.all_to_all(value, "seq", split_axis=0, concat_axis=0, tiled=True)


def shift_x(value, step):
    size = lax.axis_size("mp")
    return lax.ppermute(value, "mp", [(m, (m + 2 * step) % size) for m in range(size)])


def flip_y(value):
    size = lax.axis_size("mp")
    return lax.ppermute(value, "mp", [(m, m ^ 1) for m in range(size)])


def spread_along_x(place, keyframes, source, shape):
    piece = (keyframes.shape[0], source.shape[0], shape[1] // shape[2], HEAD)
    piece = jax.ShapeDtypeStruct(piece, BF16)
    cuts = move_call(
        functools.partial(cut_kernel, shape=shape),
        [piece] * (shape[2] - 1), place, keyframes, source,
    )
    got = [shift_x(cut, step) for step, cut in enumerate(cuts, 1)]
    return move_call(
        functools.partial(pick_x_kernel, shape=shape),
        [piece], place, keyframes, source, *got,
    )[0]


def spread_from_x(place, keyframes, mine, shape):
    other = flip_y(mine)
    (mine,) = move_call(
        functools.partial(pick_y_kernel, shape=shape),
        [jax.ShapeDtypeStruct(mine.shape, BF16)], place, keyframes, mine, other,
    )
    return [mine] + [shift_x(mine, step) for step in range(1, shape[2])]


def local(queries, keys, values, inject, keyframes, key_mask):
    queries, keys, values = queries[0], keys[0], values[0]
    frames, rows, _ = queries.shape
    shape = (frames, rows, lax.axis_size("mp") // 2)
    place = lax.axis_index("mp").astype(jnp.int32).reshape(1)
    partner_keys = swap_branch(keys)
    partner_queries = swap_branch(queries)

    value_rows = split_heads(values).reshape(-1, frames * rows, HEAD)
    value_heads = to_heads(value_rows)
    value_mine = spread_along_x(place, keyframes, value_heads, shape)
    value_extra = spread_from_x(place, keyframes, value_mine, shape)

    key_rows = blend_heads(inject, keys, partner_keys)
    key_heads = to_heads(key_rows)
    key_mine = spread_along_x(place, keyframes, key_heads, shape)
    key_extra = spread_from_x(place, keyframes, key_mine, shape)

    query_rows = blend_heads(inject, queries, partner_queries)
    query_heads = to_heads(query_rows)
    outs = []
    always = jnp.ones((1,), jnp.int32)
    for f in range(frames):
        masks = lax.dynamic_index_in_dim(key_mask, place[0] * frames + f, 0, keepdims=False)
        valid = jnp.concatenate([always, masks])
        heads = (query_heads, key_heads, value_heads)
        extra = (key_extra, value_extra)
        if f == 0:
            own = attend("own", f, rows, always, *heads)
            out = attend("more", f, rows, valid, *heads, *extra, own)
        else:
            out = attend("all", f, rows, valid, *heads, *extra)
        back = to_heads(out)
        outs.append(back.transpose(1, 0, 2).reshape(rows, -1))
    return jnp.stack(outs)[None]


def solution(mesh):
    return jax.shard_map(
        local,
        mesh=mesh,
        in_specs=(
            P("branch", "mp", "seq", None),
            P("branch", "mp", "seq", None),
            P("branch", "mp", "seq", None),
            P("branch", None),
            P(),
            P(),
        ),
        out_specs=P("branch", "mp", "seq", None),
        check_vma=False,
    )
```
